256 devices in a mesh: section: 2 (over core), seq: 32 (over z, x), head: 4 (over y).
Axes of the slice: x: 4, y: 4, z: 8, core: 2. Of those that a mesh axis runs over, the one named last changes fastest.
Arguments:
- hidden: bfloat16 [2, 16384, 4608], P('section', ('seq', 'head')), may hold values from -80 to 80
- q_weight: bfloat16 [2, 4608, 2048], P('section', None, 'head'), may hold values from -0.09375 to 0.09375
- key_value_weight: bfloat16 [4608, 2, 1024], P('seq', None, 'head'), may hold values from -0.09375 to 0.09375
- o_weight: bfloat16 [2, 2048, 4608], P('section', 'head'), may hold values from -1 to 1
- in_gain: float32 [2, 4608], P('section'), may hold values from 1 to 6
- post_gain: float32 [2, 4608], P('section'), may hold values from 0.25 to 1.75
- positions: int32 [16384], replicated, may hold values from 0 to 8191, as said below
- block_table: int32 [32, 32], replicated, may hold values from 0 to 1, as said below
Outputs:
- layer_out: bfloat16 [2, 16384, 4608], P('section', ('seq', 'head'))
The draws below stay inside these ranges and needn't reach their ends.
Inputs may be any that keep to these rules, and one draw needn't show every extreme that they name: Tokens form consecutive documents; positions start at 0 at each document's first token and rise by 1; one document has exactly 8192 tokens and none has more; there are at most 15 documents. block_table[i][j] is 1 exactly when j <= i and some token of block i and some token of block j lie in one document of the positions drawn with it; blocks are 512 consecutive tokens.
All inputs are finite; a program needn't handle non-finite values.
Results may differ from the reference program's by a relative error of at most 0.0075.
Values may be sent and summed in bfloat16 or wider, within the bound.
A program may use at most 128 MiB of HBM per device.

```python
import math
import jax
import jax.numpy as jnp
from jax import lax

MODEL_WIDTH = 4608
QUERY_HEADS = 16
VALUE_HEADS = 8
HEAD_WIDTH = 128
TOKENS_PER_SHARD = 512
CUTS = 12
TOKEN_COUNT = 16384
MOST = 8192
TOKEN_BLOCKS = 32
HQ_DEV = 4


def document_layout(key):
    base = jax.random.fold_in(key, 17)
    key_first, key_second, key_third, key_fourth, key_fifth = jax.random.split(base, 5)
    remaining = TOKEN_COUNT - MOST
    offset = jax.random.randint(key_first, (), 0, remaining + 1).astype(jnp.int32)
    loose_points = jax.random.randint(key_third, (CUTS,), 1, TOKEN_COUNT).astype(jnp.int32)
    edge_points = (jax.random.randint(key_fourth, (CUTS,), 1, TOKEN_BLOCKS) * TOKENS_PER_SHARD).astype(jnp.int32)
    on_edge = jax.random.randint(key_fifth, (CUTS,), 0, 2).astype(jnp.int32)
    cut_points = jnp.where(on_edge == 1, edge_points, loose_points).astype(jnp.int32)
    keep_cut = jax.random.randint(key_second, (CUTS,), 0, 2).astype(jnp.int32)
    inside = (cut_points >= offset) & (cut_points < offset + MOST)
    cut_points = jnp.where(inside | (keep_cut == 0), 0, cut_points)
    starts = jnp.concatenate([cut_points, jnp.stack([jnp.zeros((), jnp.int32), offset, offset + MOST])]).astype(jnp.int32)
    token_index = jnp.arange(TOKEN_COUNT, dtype=jnp.int32)
    document_start = jnp.max(jnp.where(starts[None, :] <= token_index[:, None], starts[None, :], 0), axis=1)
    return ((token_index - document_start).astype(jnp.int32), document_start.astype(jnp.int32))


def draw_positions(key, part):
    return document_layout(key)[0]


def draw_block_table(key, part):
    document_start = document_layout(key)[1].reshape(TOKEN_BLOCKS, TOKENS_PER_SHARD)
    first_start = document_start[:, 0]
    last_start = document_start[:, -1]
    row_number = jnp.arange(TOKEN_BLOCKS, dtype=jnp.int32)[:, None]
    column_number = jnp.arange(TOKEN_BLOCKS, dtype=jnp.int32)[None, :]
    linked = (column_number == row_number) | (column_number < row_number) & (last_start[None, :] == first_start[:, None])
    return linked.astype(jnp.int32)


def draw_hidden(key, part):
    key_rows, key_columns, key_noise = jax.random.split(jax.random.fold_in(key, 3), 3)
    row_scale = 0.3 * jnp.exp(jax.random.uniform(key_rows, (2, TOKEN_COUNT, 1), minval=0.0, maxval=math.log(10.0)))
    column_scale = 0.3 * jnp.exp(jax.random.uniform(key_columns, (1, 1, MODEL_WIDTH), minval=0.0, maxval=math.log(10.0)))
    noise = jnp.clip(jax.random.normal(key_noise, (2, TOKEN_COUNT, MODEL_WIDTH)), -8.0, 8.0)
    return (noise * row_scale * column_scale).astype(jnp.bfloat16)


def draw_o_weight(key, part):
    key_noise, key_columns = jax.random.split(jax.random.fold_in(key, 5), 2)
    column_scale = 0.3 * jnp.exp(jax.random.uniform(key_columns, (1, 1, MODEL_WIDTH), minval=0.0, maxval=math.log(10.0)))
    noise = jnp.clip(jax.random.normal(key_noise, (2, QUERY_HEADS * HEAD_WIDTH, MODEL_WIDTH)), -7.0, 7.0)
    return (noise * column_scale / math.sqrt(QUERY_HEADS * HEAD_WIDTH)).astype(jnp.bfloat16)


def steps_of(rng, dims, pieces, least, largest):
    def one(axis_at, parts):
        draws = jax.random.uniform(jax.random.fold_in(jax.random.fold_in(rng, 6), axis_at), (parts,), jnp.float32, least / len(pieces), largest / len(pieces))
        return jnp.repeat(jnp.exp(draws), dims[axis_at] // parts).reshape((-1,) + (1,) * (len(dims) - axis_at - 1))

    loudness = one(*pieces[0])
    for cut in pieces[1:]:
        loudness = loudness * one(*cut)
    return loudness


def centred(key, shape, width, reach, cuts=(), kind=jnp.bfloat16):
    entries = jax.random.normal(key, shape, jnp.float32) * width
    if len(cuts) > 0:
        entries = steps_of(key, shape, cuts, -0.22, 0.18) * entries
    return jnp.clip(entries, min=-reach, max=reach).astype(kind)


def setup_inputs(seed: int = 0) -> dict:
    splits = jax.random.split(jax.random.key(seed), 9)
    hidden = draw_hidden(jax.random.fold_in(splits[8], 71), 0)
    q_weight = centred(splits[1], (2, MODEL_WIDTH, QUERY_HEADS * HEAD_WIDTH), MODEL_WIDTH ** -0.5, 0.09375, ((0, 2), (2, 4)))
    key_value_weight = centred(splits[2], (MODEL_WIDTH, 2, VALUE_HEADS * HEAD_WIDTH), MODEL_WIDTH ** -0.5, 0.09375, ((0, 32), (2, 4)))
    o_weight = draw_o_weight(jax.random.fold_in(splits[8], 71), 0)
    in_gain = jnp.clip(jnp.exp(math.log(6.0) - 1.7917595 * jax.random.uniform(splits[4], (2, MODEL_WIDTH), jnp.float32) ** steps_of(splits[4], (2, MODEL_WIDTH), ((0, 2),), -0.2, 0.2)), 1.0, 6.0)
    post_gain = jnp.clip(1.0 + 0.15 * jax.random.normal(splits[5], (2, MODEL_WIDTH), jnp.float32), 0.25, 1.75)
    positions = draw_positions(jax.random.fold_in(splits[8], 71), 0)
    block_table = draw_block_table(jax.random.fold_in(splits[8], 71), 0)
    return {"hidden": hidden, "q_weight": q_weight, "key_value_weight": key_value_weight, "o_weight": o_weight, "in_gain": in_gain, "post_gain": post_gain, "positions": positions, "block_table": block_table}


epsilon = 1e-06
softcap_limit = 50.0
query_scale = 144.0 ** (-0.5)

def normalize(values):
    return values * lax.rsqrt(lax.optimization_barrier(jnp.mean(values * values, axis=-1, keepdims=True)) + epsilon)

def apply_rotation(values, token_positions):
    half_size = values.shape[-1] // 2
    frequency = 10000.0 ** (-(jnp.arange(half_size, dtype=jnp.float32) * 2.0 / values.shape[-1]))
    angles = token_positions.astype(jnp.float32)[:, None] * frequency[None, :]
    cosine = jnp.cos(angles)[:, None, :]
    sine_part = jnp.sin(angles)[:, None, :]
    first_half = values[..., :half_size]
    second_half = values[..., half_size:]
    return jnp.concatenate([first_half * cosine - second_half * sine_part, second_half * cosine + first_half * sine_part], axis=-1)

def attend_all(query_matrix, common_key_rows, common_value_rows, document_start, block_table):
    queries_per_group = QUERY_HEADS // VALUE_HEADS
    grouped_queries = query_matrix.reshape(TOKEN_BLOCKS, TOKENS_PER_SHARD, VALUE_HEADS, queries_per_group, HEAD_WIDTH)

    def one_block(block_number):
        query_block = lax.dynamic_index_in_dim(grouped_queries, block_number, 0, keepdims=False).astype(jnp.float32)
        query_index = block_number * TOKENS_PER_SHARD + jnp.arange(TOKENS_PER_SHARD, dtype=jnp.int32)
        query_start = lax.dynamic_slice_in_dim(document_start, block_number * TOKENS_PER_SHARD, TOKENS_PER_SHARD)

        def visit_block(running, key_block):

            def compute(accumulated):
                numerator, denominator = accumulated
                first_row = key_block * TOKENS_PER_SHARD
                key_rows = lax.dynamic_slice_in_dim(common_key_rows, first_row, TOKENS_PER_SHARD, 0).astype(jnp.float32)
                value_rows = lax.dynamic_slice_in_dim(common_value_rows, first_row, TOKENS_PER_SHARD, 0).astype(jnp.float32)
                key_index = first_row + jnp.arange(TOKENS_PER_SHARD, dtype=jnp.int32)
                key_start = lax.dynamic_slice_in_dim(document_start, first_row, TOKENS_PER_SHARD)
                scores = jnp.einsum('qhgd,khd->hgqk', query_block, key_rows) * query_scale
                capped = softcap_limit * jnp.tanh(scores / softcap_limit)
                visible = (key_index[None, :] <= query_index[:, None]) & (key_start[None, :] == query_start[:, None])
                raised = jnp.where(visible, jnp.exp(capped), 0.0)
                probs = lax.optimization_barrier(raised.astype(jnp.bfloat16)).astype(jnp.float32)
                numerator = numerator + jnp.einsum('hgqk,khd->hgqd', probs, value_rows)
                denominator = denominator + lax.optimization_barrier(jnp.sum(raised, axis=-1))
                return (numerator, denominator)
            allowed = (key_block <= block_number) & (block_table[block_number, key_block] == 1)
            return (lax.cond(allowed, compute, lambda accumulated: accumulated, running), None)
        initial_state = (jnp.zeros((VALUE_HEADS, queries_per_group, TOKENS_PER_SHARD, HEAD_WIDTH), jnp.float32), jnp.zeros((VALUE_HEADS, queries_per_group, TOKENS_PER_SHARD), jnp.float32))
        (numerator, denominator), _ = lax.scan(visit_block, initial_state, jnp.arange(TOKEN_BLOCKS, dtype=jnp.int32))
        result = numerator / denominator[..., None]
        return jnp.transpose(result, (2, 0, 1, 3)).reshape(TOKENS_PER_SHARD, QUERY_HEADS * HEAD_WIDTH).astype(jnp.bfloat16)
    return lax.map(one_block, jnp.arange(TOKEN_BLOCKS, dtype=jnp.int32)).reshape(TOKEN_COUNT, QUERY_HEADS * HEAD_WIDTH)

def reference(hidden, q_weight, key_value_weight, o_weight, in_gain, post_gain, positions, block_table):
    token_index = jnp.arange(TOKEN_COUNT, dtype=jnp.int32)
    document_start = token_index - positions
    results = []
    common_key_rows = None
    common_value_rows = None
    group_columns = HQ_DEV * HEAD_WIDTH
    for section_index in range(2):
        residual = hidden[section_index].astype(jnp.float32)
        normed = (normalize(residual) * in_gain[section_index]).astype(jnp.bfloat16)
        query_matrix = jnp.dot(normed, q_weight[section_index], preferred_element_type=jnp.float32)
        query_matrix = apply_rotation(query_matrix.reshape(TOKEN_COUNT, QUERY_HEADS, HEAD_WIDTH), positions).astype(jnp.bfloat16)
        if section_index == 0:
            projected_rows = jnp.einsum('td,dce->tce', normed.astype(jnp.float32), key_value_weight.astype(jnp.float32))
            common_key_rows = apply_rotation(projected_rows[:, 0].reshape(TOKEN_COUNT, VALUE_HEADS, HEAD_WIDTH), positions).astype(jnp.bfloat16)
            common_value_rows = projected_rows[:, 1].reshape(TOKEN_COUNT, VALUE_HEADS, HEAD_WIDTH).astype(jnp.bfloat16)
        attended = attend_all(query_matrix, common_key_rows, common_value_rows, document_start, block_table)
        summed = jnp.zeros((TOKEN_COUNT, MODEL_WIDTH), jnp.float32)
        for group_number in range(QUERY_HEADS // HQ_DEV):
            low = group_number * group_columns
            group_term = jnp.dot(attended[:, low:low + group_columns], o_weight[section_index, low:low + group_columns], preferred_element_type=jnp.float32)
            summed = summed + lax.optimization_barrier(group_term.astype(jnp.bfloat16)).astype(jnp.float32)
        layer_rows = residual + normalize(summed) * post_gain[section_index]
        results.append(layer_rows.astype(jnp.bfloat16))
    return jnp.stack(results)
```

```python
import math

import functools

import jax
import jax.numpy as jnp
from jax import lax
from jax.experimental import pallas as pl
from jax.experimental.pallas import tpu as pltpu
from jax.sharding import PartitionSpec as P

HEAD_WIDTH = 128


epsilon = 1e-06
softcap_limit = 50.0
query_scale = 144.0 ** (-0.5)
RAISE = softcap_limit * math.log2(math.e)
LONGEST = 8192


def shifted(value, axis, steps):
    count = lax.axis_size(axis)
    first, last = (max(0, -steps), min(count, count - steps))
    return lax.ppermute(value, axis, [(source, source + steps) for source in range(first, last)])


def normalize(values):
    return values * lax.rsqrt(jnp.mean(values * values, axis=-1, keepdims=True) + epsilon)


def apply_rotation(values, token_positions):
    half_size = values.shape[-1] // 2
    frequency = 10000.0 ** (-(jnp.arange(half_size, dtype=jnp.float32) * 2.0 / values.shape[-1]))
    angles = token_positions.astype(jnp.float32)[:, None] * frequency[None, :]
    cosine = jnp.cos(angles)[:, None, :]
    sine_part = jnp.sin(angles)[:, None, :]
    first_half = values[..., :half_size]
    second_half = values[..., half_size:]
    return jnp.concatenate(
        [
            first_half * cosine - second_half * sine_part,
            second_half * cosine + first_half * sine_part,
        ],
        axis=-1,
    )


def attention_kernel(window, key_heads, meta, q_ref, kv_ref, start_ref, out_ref, total, wide):
    step = pl.program_id(0)
    rows = q_ref.shape[0]
    heads = q_ref.shape[1] // HEAD_WIDTH
    shard = meta[0]
    block = shard - step
    group = heads // key_heads

    @pl.when(step == 0)
    def _():
        total[...] = jnp.zeros_like(total)
        wide[...] = jnp.ones_like(wide)

    @pl.when(block >= meta[1])
    def _():
        listed = meta[2 + jnp.maximum(block, 0)] == 1
        start = jnp.where(listed, start_ref[:, :1], shard * rows + rows)
        keys = block * rows + lax.broadcasted_iota(jnp.int32, (rows, rows), 1)
        queries = shard * rows + lax.broadcasted_iota(jnp.int32, (rows, rows), 0)
        seen = (keys >= start) & (keys <= queries)
        for kv_head in range(key_heads):
            low = (key_heads + kv_head) * HEAD_WIDTH
            wide[kv_head, :, :HEAD_WIDTH] = kv_ref[:, low : low + HEAD_WIDTH]
        for head in range(heads):
            kv_head = head // group
            key = kv_ref[:, kv_head * HEAD_WIDTH : (kv_head + 1) * HEAD_WIDTH]
            scores = lax.dot_general(
                q_ref[:, head * HEAD_WIDTH : (head + 1) * HEAD_WIDTH],
                key,
                (((1,), (1,)), ((), ())),
                preferred_element_type=jnp.float32,
            )
            raised = jnp.where(seen, jnp.exp2(jnp.tanh(scores) * RAISE), 0.0)
            total[head] += jnp.dot(
                raised.astype(jnp.bfloat16), wide[kv_head], preferred_element_type=jnp.float32
            )

    @pl.when(step == window - 1)
    def _():
        for head in range(heads):
            value = total[head]
            out_ref[:, head * HEAD_WIDTH : (head + 1) * HEAD_WIDTH] = (
                value[:, :HEAD_WIDTH] / value[:, HEAD_WIDTH:]
            ).astype(jnp.bfloat16)


def attention(queries, incoming, starts, meta, key_heads):
    rows, columns = queries.shape
    window = LONGEST // rows + 1
    kv_columns = incoming.shape[1]
    return pl.pallas_call(
        functools.partial(attention_kernel, window, key_heads),
        out_shape=jax.ShapeDtypeStruct((rows, columns), jnp.bfloat16),
        grid_spec=pltpu.PrefetchScalarGridSpec(
            num_scalar_prefetch=1,
            grid=(window,),
            in_specs=[
                pl.BlockSpec((rows, columns), lambda j, meta: (0, 0)),
                pl.BlockSpec(
                    (rows, kv_columns), lambda j, meta: (jnp.maximum(meta[0] - j, meta[1]), 0)
                ),
                pl.BlockSpec((rows, HEAD_WIDTH), lambda j, meta: (0, 0)),
            ],
            out_specs=pl.BlockSpec((rows, columns), lambda j, meta: (0, 0)),
            scratch_shapes=[
                pltpu.VMEM((columns // HEAD_WIDTH, rows, 2 * HEAD_WIDTH), jnp.float32),
                pltpu.VMEM((key_heads, rows, 2 * HEAD_WIDTH), jnp.bfloat16),
            ],
        ),
        compiler_params=pltpu.CompilerParams(vmem_limit_bytes=56 * 2**20),
        name="attention",
    )(meta, queries, incoming, starts)


def local(hidden, q_weight, key_value_weight, o_weight, in_gain, post_gain, positions, block_table):
    section_index = lax.axis_index("section")
    shard_index = lax.axis_index("seq")
    gathered = lax.all_gather(hidden[0], "head", axis=0, tiled=True)
    local_rows = gathered.shape[0]
    first_row = shard_index * local_rows
    local_positions = lax.dynamic_slice_in_dim(positions, first_row, local_rows)
    normed = (normalize(gathered.astype(jnp.float32)) * in_gain[0]).astype(jnp.bfloat16)
    query_matrix = jnp.dot(normed, q_weight[0], preferred_element_type=jnp.float32)
    head_count = query_matrix.shape[1] // HEAD_WIDTH
    query_matrix = apply_rotation(
        query_matrix.reshape(local_rows, head_count, HEAD_WIDTH), local_positions
    )
    query_matrix = (query_matrix * (query_scale / softcap_limit)).astype(jnp.bfloat16)
    query_matrix = query_matrix.reshape(local_rows, head_count * HEAD_WIDTH)
    value_width = key_value_weight.shape[2]
    projected_rows = jnp.einsum(
        "td,dce->tce",
        normed,
        lax.all_gather(key_value_weight, "seq", axis=0, tiled=True),
        preferred_element_type=jnp.float32,
    )
    key_heads = value_width // HEAD_WIDTH
    rotated_keys = apply_rotation(
        projected_rows[:, 0].reshape(local_rows, key_heads, HEAD_WIDTH), local_positions
    )
    produced = jnp.stack(
        [rotated_keys.reshape(local_rows, value_width), projected_rows[:, 1]], axis=1
    ).astype(jnp.bfloat16)
    received = shifted(produced, "section", 1)
    shared = jnp.where(section_index == 0, produced, received)
    incoming = lax.all_gather(shared.reshape(local_rows, -1), "seq", axis=0, tiled=True)
    query_index = first_row + jnp.arange(local_rows, dtype=jnp.int32)
    query_start = query_index - local_positions
    meta = jnp.concatenate(
        [jnp.stack([shard_index, query_start[0] // local_rows]), block_table[shard_index]]
    )
    starts = jnp.broadcast_to(query_start[:, None], (local_rows, HEAD_WIDTH))
    attended = attention(query_matrix, incoming, starts, meta, key_heads)
    out_proj = o_weight[0]
    summed = lax.psum_scatter(
        jnp.dot(attended, out_proj, preferred_element_type=jnp.float32).astype(jnp.bfloat16),
        "head",
        scatter_dimension=0,
        tiled=True,
    ).astype(jnp.float32)
    residual = hidden[0].astype(jnp.float32)
    return (residual + normalize(summed) * post_gain[0]).astype(jnp.bfloat16)[None]


def solution(mesh):
    placed = (
        P("section", ("seq", "head"), None),
        P("section", None, "head"),
        P("seq", None, "head"),
        P("section", "head", None),
        P("section", None),
        P("section", None),
        P(),
        P(),
    )
    return jax.shard_map(
        local,
        mesh=mesh,
        in_specs=placed,
        out_specs=P("section", ("seq", "head"), None),
        check_vma=False,
    )
```

```python
import math

import functools

import jax
import jax.numpy as jnp
from jax import lax
from jax.experimental import pallas as pl
from jax.experimental.pallas import tpu as pltpu
from jax.sharding import PartitionSpec as P

HEAD_WIDTH = 128


epsilon = 1e-06
softcap_limit = 50.0
query_scale = 144.0 ** (-0.5)
RAISE = softcap_limit * math.log2(math.e)
XS, ZS = 4, 8


def normalize(values):
    return values * lax.rsqrt(jnp.mean(values * values, axis=-1, keepdims=True) + epsilon)


def apply_rotation(values, token_positions):
    half_size = values.shape[-1] // 2
    frequency = 10000.0 ** (-(jnp.arange(half_size, dtype=jnp.float32) * 2.0 / values.shape[-1]))
    angles = token_positions.astype(jnp.float32)[:, None] * frequency[None, :]
    cosine = jnp.cos(angles)[:, None, :]
    sine_part = jnp.sin(angles)[:, None, :]
    first_half = values[..., :half_size]
    second_half = values[..., half_size:]
    return jnp.concatenate(
        [
            first_half * cosine - second_half * sine_part,
            second_half * cosine + first_half * sine_part,
        ],
        axis=-1,
    )


SLOTS = ((0, 0), (1, 0), (1, 1), (1, 3), (2, 0), (1, 2), (2, 1), (2, 3), (3, 0), (2, 2), (3, 1), (3, 3), (4, 0), (3, 2), (-1, 1), (-1, 3), (-1, 2))


def start_copy(source, target, sent, landed, **place):
    copy = pltpu.make_async_remote_copy(
        src_ref=source,
        dst_ref=target,
        send_sem=sent,
        recv_sem=landed,
        device_id=place,
        device_id_type=pl.DeviceIdType.MESH,
    )
    return copy


def greet(places):
    barrier = pltpu.get_barrier_semaphore()
    for place in places:
        pl.semaphore_signal(
            barrier, inc=1, device_id=place, device_id_type=pl.DeviceIdType.MESH
        )
    pl.semaphore_wait(barrier, len(places))


def attention_kernel(
    meta, q_ref, kv_ref, start_ref, out_ref,
    queries, blocks, total, wide, ready, landing,
    swap_s, swap_r, own_s, z_s, z_r, right_s, right_r, left_s, left_r, key_s, key_r, value_s, value_r, far_s, far_r,
):
    section = lax.axis_index("section")
    shard = lax.axis_index("seq")
    z, x = shard // XS, shard % XS
    other = 1 - section
    rows = start_ref.shape[0]
    up = ((z + 1) % ZS) * XS + x
    down = ((z + ZS - 1) % ZS) * XS + x
    right = z * XS + (x + 1) % XS
    left = z * XS + (x + 3) % XS
    far = z * XS + (x + 2) % XS
    greet([{"section": other}, {"seq": up}, {"seq": down}, {"seq": right}, {"seq": left}, {"seq": far}])

    def swap_queries():
        return start_copy(
            q_ref.at[pl.ds(2 * other, 2)], queries.at[pl.ds(2 * section, 2)],
            swap_s.at[0], swap_r.at[0], section=other,
        )

    def hand_keys():
        return start_copy(kv_ref.at[1], blocks.at[0], swap_s.at[1], swap_r.at[1], section=other)

    def climb(step):
        slots = (0, 1, 4, 8, 12)
        return start_copy(
            blocks.at[slots[step]], blocks.at[slots[step + 1]], z_s.at[step], z_r.at[step], seq=up
        )

    def to_right(row):
        source, target = ((1, 2), (4, 6), (8, 10))[row]
        return start_copy(blocks.at[source], blocks.at[target], right_s.at[row], right_r.at[row], seq=right)

    def to_left(row):
        source, target = ((1, 3), (4, 7), (8, 11))[row]
        return start_copy(blocks.at[source], blocks.at[target], left_s.at[row], left_r.at[row], seq=left)

    def pass_keys(row):
        source, target = ((2, 5), (6, 9), (10, 13))[row]
        columns = pl.ds(0, HEAD_WIDTH)
        return start_copy(
            blocks.at[source, :, columns], blocks.at[target, :, columns], key_s.at[row], key_r.at[row], seq=right
        )

    def pass_values(row):
        source, target = ((3, 5), (7, 9), (11, 13))[row]
        columns = pl.ds(HEAD_WIDTH, HEAD_WIDTH)
        return start_copy(
            blocks.at[source, :, columns], blocks.at[target, :, columns], value_s.at[row], value_r.at[row], seq=left
        )

    def edge_right(source):
        return start_copy(blocks.at[source], blocks.at[14], right_s.at[3], right_r.at[3], seq=right)

    def edge_left(source):
        return start_copy(blocks.at[source], blocks.at[15], left_s.at[3], left_r.at[3], seq=left)

    def edge_far(source):
        return start_copy(blocks.at[source], blocks.at[16], far_s.at[0], far_r.at[0], seq=far)

    own_queries = pltpu.make_async_copy(
        q_ref.at[pl.ds(2 * section, 2)], queries.at[pl.ds(2 * section, 2)], own_s.at[0]
    )
    own_keys = pltpu.make_async_copy(kv_ref.at[0], blocks.at[0], own_s.at[1])
    swap_queries().start()
    own_queries.start()

    @pl.when(section == 0)
    def _():
        hand_keys().start()
        own_keys.start()

    total[...] = jnp.zeros_like(total)
    wide[...] = jnp.ones_like(wide)

    @pl.when(section == 0)
    def _():
        own_keys.wait()

    @pl.when(section == 1)
    def _():
        hand_keys().wait_recv()

    climb(0).start()
    pl.when(x < 3)(lambda: edge_right(0).start())
    pl.when(x == 0)(lambda: edge_left(0).start())
    pl.when(x < 2)(lambda: edge_far(0).start())
    own_queries.wait()
    swap_queries().wait_recv()

    def turn(step):
        if step == 1:
            climb(0).wait_recv()
            climb(1).start()
            to_right(0).start()
            to_left(0).start()
        elif step in (2, 6, 10):
            row = (step - 2) // 4
            to_right(row).wait_recv()
            pass_keys(row).start()
            to_left(row).wait_recv()
            pass_values(row).start()
            climb(row + 1).wait_recv()
            if row < 2:
                climb(row + 2).start()
                to_right(row + 1).start()
                to_left(row + 1).start()
            else:
                pl.when(x == 3)(lambda: edge_right(12).start())
                pl.when(x > 0)(lambda: edge_left(12).start())
                pl.when(x > 1)(lambda: edge_far(12).start())
        elif step in (5, 9, 13):
            row = (step - 5) // 4
            pass_keys(row).wait_recv()
            pass_values(row).wait_recv()
        elif step == 14:
            edge_right(0).wait_recv()
        elif step == 15:
            edge_left(0).wait_recv()
        elif step == 16:
            edge_far(0).wait_recv()

    def visit(step, carried):
        for number in (1, 2, 5, 6, 9, 10, 13, 14, 15, 16):
            pl.when(step == number)(functools.partial(turn, number))
        first = meta[0, step]
        listed = meta[1, step] == 1
        start = jnp.where(listed, start_ref[:, :1], shard * rows + rows)
        keys = first + lax.broadcasted_iota(jnp.int32, (rows, rows), 1)
        own = shard * rows + lax.broadcasted_iota(jnp.int32, (rows, rows), 0)
        seen = (keys >= start) & (keys <= own)
        wide[:, :HEAD_WIDTH] = blocks[step, :, HEAD_WIDTH:]
        for head in range(4):
            scores = lax.dot_general(
                queries[head],
                blocks[step, :, :HEAD_WIDTH],
                (((1,), (1,)), ((), ())),
                preferred_element_type=jnp.float32,
            )
            raised = jnp.where(seen, jnp.exp2(jnp.tanh(scores) * RAISE), 0.0)
            total[head] += jnp.dot(
                raised.astype(jnp.bfloat16), wide[...], preferred_element_type=jnp.float32
            )
        return carried

    lax.fori_loop(0, len(SLOTS), visit, 0)

    for mine in range(2):
        value = total[2 * other + mine]
        ready[:, mine * HEAD_WIDTH : (mine + 1) * HEAD_WIDTH] = (
            value[:, :HEAD_WIDTH] / value[:, HEAD_WIDTH:]
        ).astype(jnp.bfloat16)
    swap_back = start_copy(ready, landing, swap_s.at[2], swap_r.at[2], section=other)
    swap_back.start()
    for mine in range(2):
        value = total[2 * section + mine]
        out_ref[section, :, mine * HEAD_WIDTH : (mine + 1) * HEAD_WIDTH] = (
            value[:, :HEAD_WIDTH] / value[:, HEAD_WIDTH:]
        ).astype(jnp.bfloat16)
    swap_back.wait_recv()
    out_ref[other] = landing[...]
    swap_back.wait_send()
    swap_queries().wait_send()
    pl.when(section == 0)(lambda: hand_keys().wait_send())
    for step in range(4):
        climb(step).wait_send()
    for row in range(3):
        to_right(row).wait_send()
        to_left(row).wait_send()
        pass_keys(row).wait_send()
        pass_values(row).wait_send()
    edge_right(0).wait_send()
    edge_left(0).wait_send()
    edge_far(0).wait_send()


def attention(queries, own_kv, starts, meta):
    rows = starts.shape[0]
    dma = pltpu.SemaphoreType.DMA
    whole = pl.BlockSpec(memory_space=pltpu.VMEM)
    return pl.pallas_call(
        attention_kernel,
        out_shape=jax.ShapeDtypeStruct((2, rows, 2 * HEAD_WIDTH), jnp.bfloat16),
        in_specs=[pl.BlockSpec(memory_space=pltpu.SMEM), whole, whole, whole],
        out_specs=whole,
        scratch_shapes=[
            pltpu.VMEM((4, rows, HEAD_WIDTH), jnp.bfloat16),
            pltpu.VMEM((len(SLOTS), rows, 2 * HEAD_WIDTH), jnp.bfloat16),
            pltpu.VMEM((4, rows, 2 * HEAD_WIDTH), jnp.float32),
            pltpu.VMEM((rows, 2 * HEAD_WIDTH), jnp.bfloat16),
            pltpu.VMEM((rows, 2 * HEAD_WIDTH), jnp.bfloat16),
            pltpu.VMEM((rows, 2 * HEAD_WIDTH), jnp.bfloat16),
            dma((3,)), dma((3,)), dma((2,)),
            dma((4,)), dma((4,)), dma((4,)), dma((4,)), dma((4,)), dma((4,)),
            dma((3,)), dma((3,)), dma((3,)), dma((3,)), dma((1,)), dma((1,)),
        ],
        compiler_params=pltpu.CompilerParams(
            collective_id=1, has_side_effects=True, vmem_limit_bytes=56 * 2**20
        ),
        name="attention",
    )(meta, queries, own_kv, starts)


PIECES = 3


def mix_kernel(
    heads_ref, weight_hbm, hidden_ref, gain_ref, out_ref,
    weight, far_out, near_out, sum_out, far_in, near_in, sum_in, mixed,
    load, far_s, far_r, near_s, near_r, sum_s, sum_r,
):
    place = lax.axis_index("head")
    count = 4
    sides = ((place + 1) % count, (place + 3) % count)
    opposite = (place + 2) % count
    rows, width = mixed.shape
    half = width // 2
    piece = half // PIECES
    fetch = pltpu.make_async_copy(weight_hbm, weight, load.at[0])
    fetch.start()
    greet([{"head": sides[0]}, {"head": sides[1]}])
    fetch.wait()
    depth = heads_ref.shape[2]

    def partial(target, low):
        span = pl.ds(pl.multiple_of(target * rows, rows), rows)
        return jnp.dot(
            heads_ref[0, span, :], weight[:depth, low : low + piece], preferred_element_type=jnp.float32
        ) + jnp.dot(
            heads_ref[1, span, :], weight[depth:, low : low + piece], preferred_element_type=jnp.float32
        )

    def send(source, target, sent, landed, side, part):
        return start_copy(
            source.at[side, part], target.at[side, part], sent.at[side, part], landed.at[side, part],
            head=sides[side],
        )

    def far_copy(side, part):
        return send(far_out, far_in, far_s, far_r, side, part)

    def near_copy(side, part):
        return send(near_out, near_in, near_s, near_r, side, part)

    def sum_copy(side, part):
        return send(sum_out, sum_in, sum_s, sum_r, side, part)

    for part in range(PIECES):
        for side in range(2):
            low = side * half + part * piece
            far_out[side, part] = partial(opposite, low).astype(jnp.bfloat16)
            far_copy(side, part).start()
    for part in range(PIECES):
        for side in range(2):
            low = (1 - side) * half + part * piece
            near_out[side, part] = partial(sides[side], low).astype(jnp.bfloat16)
            near_copy(side, part).start()
    for part in range(PIECES):
        for side in range(2):
            low = side * half + part * piece
            own = partial(sides[side], low).astype(jnp.bfloat16).astype(jnp.float32)
            far_copy(side, part).wait_recv()
            sum_out[side, part] = (own + far_in[side, part].astype(jnp.float32)).astype(jnp.bfloat16)
            sum_copy(side, part).start()
    for part in range(2 * PIECES):
        low = part * piece
        mixed[:, low : low + piece] = partial(place, low).astype(jnp.bfloat16).astype(jnp.float32)
    for part in range(PIECES):
        for side in range(2):
            low = (1 - side) * half + part * piece
            near_copy(side, part).wait_recv()
            mixed[:, low : low + piece] += near_in[side, part].astype(jnp.float32)
    squares = jnp.zeros((rows, 128), jnp.float32)
    for part in range(PIECES):
        for side in range(2):
            low = side * half + part * piece
            sum_copy(side, part).wait_recv()
            value = mixed[:, low : low + piece] + sum_in[side, part].astype(jnp.float32)
            mixed[:, low : low + piece] = value
            square = value * value
            for column in range(0, piece, 128):
                squares = squares + square[:, column : column + 128]
    scale = lax.rsqrt(jnp.sum(squares, axis=-1, keepdims=True) / width + epsilon)
    for part in range(2 * PIECES):
        span = slice(part * piece, (part + 1) * piece)
        out_ref[:, span] = (
            hidden_ref[:, span].astype(jnp.float32) + mixed[:, span] * scale * gain_ref[:, span]
        ).astype(jnp.bfloat16)
    for part in range(PIECES):
        for side in range(2):
            far_copy(side, part).wait_send()
            near_copy(side, part).wait_send()
            sum_copy(side, part).wait_send()


def mix(heads, weight, hidden, gain):
    rows, width = hidden.shape
    dma = pltpu.SemaphoreType.DMA
    whole = pl.BlockSpec(memory_space=pltpu.VMEM)
    slots = pltpu.VMEM((2, PIECES, rows, width // (2 * PIECES)), jnp.bfloat16)
    return pl.pallas_call(
        mix_kernel,
        out_shape=jax.ShapeDtypeStruct((rows, width), jnp.bfloat16),
        in_specs=[whole, pl.BlockSpec(memory_space=pl.ANY), whole, whole],
        out_specs=whole,
        scratch_shapes=[
            pltpu.VMEM(weight.shape, jnp.bfloat16),
            slots, slots, slots, slots, slots, slots,
            pltpu.VMEM((rows, width), jnp.float32),
            dma((1,)),
        ]
        + [dma((2, PIECES))] * 6,
        compiler_params=pltpu.CompilerParams(
            collective_id=2, has_side_effects=True, vmem_limit_bytes=56 * 2**20
        ),
        name="mix",
    )(heads, weight, hidden, gain)


def visits(shard, rows, block_table):
    z, x = shard // XS, shard % XS
    back = jnp.array([row for row, _ in SLOTS], jnp.int32)
    aside = jnp.array([column for _, column in SLOTS], jnp.int32)
    source = (x + XS - aside) % XS
    back = jnp.where(back < 0, jnp.where(source < x, 0, 4), back)
    block = (z - back) * XS + source
    listed = block_table[shard][jnp.maximum(block, 0)]
    return jnp.stack([block * rows, listed])


def local(hidden, q_weight, key_value_weight, o_weight, in_gain, post_gain, positions, block_table):
    shard_index = lax.axis_index("seq")
    gathered = lax.all_gather(hidden[0], "head", axis=0, tiled=True)
    local_rows = gathered.shape[0]
    first_row = shard_index * local_rows
    local_positions = lax.dynamic_slice_in_dim(positions, first_row, local_rows)
    normed = (normalize(gathered.astype(jnp.float32)) * in_gain[0]).astype(jnp.bfloat16)
    query_matrix = jnp.dot(normed, q_weight[0], preferred_element_type=jnp.float32)
    head_count = query_matrix.shape[1] // HEAD_WIDTH
    query_matrix = apply_rotation(
        query_matrix.reshape(local_rows, head_count, HEAD_WIDTH), local_positions
    )
    query_matrix = (query_matrix * (query_scale / softcap_limit)).astype(jnp.bfloat16)
    query_matrix = jnp.transpose(query_matrix, (1, 0, 2))
    value_width = key_value_weight.shape[2]
    projected_rows = jnp.einsum(
        "td,dce->tce",
        normed,
        lax.all_gather(key_value_weight, "seq", axis=0, tiled=True),
        preferred_element_type=jnp.float32,
    )
    key_heads = value_width // HEAD_WIDTH
    rotated_keys = apply_rotation(
        projected_rows[:, 0].reshape(local_rows, key_heads, HEAD_WIDTH), local_positions
    )
    own_kv = jnp.stack(
        [
            jnp.concatenate(
                [rotated_keys[:, head], projected_rows[:, 1, head * HEAD_WIDTH : (head + 1) * HEAD_WIDTH]],
                axis=1,
            )
            for head in range(key_heads)
        ]
    ).astype(jnp.bfloat16)
    query_index = first_row + jnp.arange(local_rows, dtype=jnp.int32)
    starts = jnp.broadcast_to((query_index - local_positions)[:, None], (local_rows, HEAD_WIDTH))
    attended = attention(query_matrix, own_kv, starts, visits(shard_index, local_rows, block_table))
    return mix(attended, o_weight[0], hidden[0], post_gain)[None]


def solution(mesh):
    placed = (
        P("section", ("seq", "head"), None),
        P("section", None, "head"),
        P("seq", None, "head"),
        P("section", "head", None),
        P("section", None),
        P("section", None),
        P(),
        P(),
    )
    return jax.shard_map(
        local,
        mesh=mesh,
        in_specs=placed,
        out_specs=P("section", ("seq", "head"), None),
        check_vma=False,
    )
```

```python
import math

import functools

import jax
import jax.numpy as jnp
from jax import lax
from jax.experimental import pallas as pl
from jax.experimental.pallas import tpu as pltpu
from jax.sharding import PartitionSpec as P

HEAD_WIDTH = 128


epsilon = 1e-06
softcap_limit = 50.0
query_scale = 144.0 ** (-0.5)
RAISE = softcap_limit * math.log2(math.e)
XS, ZS = 4, 8


SLOTS = ((0, 0), (1, 0), (1, 1), (1, 3), (2, 0), (1, 2), (2, 1), (2, 3), (3, 0), (2, 2), (3, 1), (3, 3), (4, 0), (3, 2), (-1, 1), (-1, 3), (-1, 2))


def start_copy(source, target, sent, landed, **place):
    copy = pltpu.make_async_remote_copy(
        src_ref=source,
        dst_ref=target,
        send_sem=sent,
        recv_sem=landed,
        device_id=place,
        device_id_type=pl.DeviceIdType.MESH,
    )
    return copy


def greet(places):
    barrier = pltpu.get_barrier_semaphore()
    for place in places:
        pl.semaphore_signal(
            barrier, inc=1, device_id=place, device_id_type=pl.DeviceIdType.MESH
        )
    pl.semaphore_wait(barrier, len(places))


def attention_kernel(
    meta, q_ref, kv_ref, start_ref, out_ref,
    queries, blocks, total, wide, ready, landing,
    swap_s, swap_r, own_s, z_s, z_r, right_s, right_r, left_s, left_r, key_s, key_r, value_s, value_r, far_s, far_r,
):
    section = lax.axis_index("section")
    shard = lax.axis_index("seq")
    z, x = shard // XS, shard % XS
    other = 1 - section
    rows = start_ref.shape[0]
    up = ((z + 1) % ZS) * XS + x
    down = ((z + ZS - 1) % ZS) * XS + x
    right = z * XS + (x + 1) % XS
    left = z * XS + (x + 3) % XS
    far = z * XS + (x + 2) % XS
    greet([{"section": other}, {"seq": up}, {"seq": down}, {"seq": right}, {"seq": left}, {"seq": far}])

    def swap_queries():
        return start_copy(
            q_ref.at[pl.ds(2 * other, 2)], queries.at[pl.ds(2 * section, 2)],
            swap_s.at[0], swap_r.at[0], section=other,
        )

    def hand_keys():
        return start_copy(kv_ref.at[1], blocks.at[0], swap_s.at[1], swap_r.at[1], section=other)

    def climb(step):
        slots = (0, 1, 4, 8, 12)
        return start_copy(
            blocks.at[slots[step]], blocks.at[slots[step + 1]], z_s.at[step], z_r.at[step], seq=up
        )

    def to_right(row):
        source, target = ((1, 2), (4, 6), (8, 10))[row]
        return start_copy(blocks.at[source], blocks.at[target], right_s.at[row], right_r.at[row], seq=right)

    def to_left(row):
        source, target = ((1, 3), (4, 7), (8, 11))[row]
        return start_copy(blocks.at[source], blocks.at[target], left_s.at[row], left_r.at[row], seq=left)

    def pass_keys(row):
        source, target = ((2, 5), (6, 9), (10, 13))[row]
        columns = pl.ds(0, HEAD_WIDTH)
        return start_copy(
            blocks.at[source, :, columns], blocks.at[target, :, columns], key_s.at[row], key_r.at[row], seq=right
        )

    def pass_values(row):
        source, target = ((3, 5), (7, 9), (11, 13))[row]
        columns = pl.ds(HEAD_WIDTH, HEAD_WIDTH)
        return start_copy(
            blocks.at[source, :, columns], blocks.at[target, :, columns], value_s.at[row], value_r.at[row], seq=left
        )

    def edge_right(source):
        return start_copy(blocks.at[source], blocks.at[14], right_s.at[3], right_r.at[3], seq=right)

    def edge_left(source):
        return start_copy(blocks.at[source], blocks.at[15], left_s.at[3], left_r.at[3], seq=left)

    def edge_far(source):
        return start_copy(blocks.at[source], blocks.at[16], far_s.at[0], far_r.at[0], seq=far)

    own_queries = pltpu.make_async_copy(
        q_ref.at[pl.ds(2 * section, 2)], queries.at[pl.ds(2 * section, 2)], own_s.at[0]
    )
    own_keys = pltpu.make_async_copy(kv_ref.at[0], blocks.at[0], own_s.at[1])
    swap_queries().start()
    own_queries.start()

    @pl.when(section == 0)
    def _():
        hand_keys().start()
        own_keys.start()

    total[...] = jnp.zeros_like(total)
    wide[...] = jnp.ones_like(wide)

    @pl.when(section == 0)
    def _():
        own_keys.wait()

    @pl.when(section == 1)
    def _():
        hand_keys().wait_recv()

    climb(0).start()
    pl.when(x < 3)(lambda: edge_right(0).start())
    pl.when(x == 0)(lambda: edge_left(0).start())
    pl.when(x < 2)(lambda: edge_far(0).start())
    own_queries.wait()
    swap_queries().wait_recv()

    def turn(step):
        if step == 1:
            climb(0).wait_recv()
            climb(1).start()
            to_right(0).start()
            to_left(0).start()
        elif step in (2, 6, 10):
            row = (step - 2) // 4
            to_right(row).wait_recv()
            pass_keys(row).start()
            to_left(row).wait_recv()
            pass_values(row).start()
            climb(row + 1).wait_recv()
            if row < 2:
                climb(row + 2).start()
                to_right(row + 1).start()
                to_left(row + 1).start()
            else:
                pl.when(x == 3)(lambda: edge_right(12).start())
                pl.when(x > 0)(lambda: edge_left(12).start())
                pl.when(x > 1)(lambda: edge_far(12).start())
        elif step in (5, 9, 13):
            row = (step - 5) // 4
            pass_keys(row).wait_recv()
            pass_values(row).wait_recv()
        elif step == 14:
            edge_right(0).wait_recv()
        elif step == 15:
            edge_left(0).wait_recv()
        elif step == 16:
            edge_far(0).wait_recv()

    def visit(step, carried):
        for number in (1, 2, 5, 6, 9, 10, 13, 14, 15, 16):
            pl.when(step == number)(functools.partial(turn, number))
        first = meta[0, step]
        listed = meta[1, step] == 1
        start = jnp.where(listed, start_ref[:, :1], shard * rows + rows)
        keys = first + lax.broadcasted_iota(jnp.int32, (rows, rows), 1)
        own = shard * rows + lax.broadcasted_iota(jnp.int32, (rows, rows), 0)
        seen = (keys >= start) & (keys <= own)
        wide[:, :HEAD_WIDTH] = blocks[step, :, HEAD_WIDTH:]
        for head in range(4):
            scores = lax.dot_general(
                queries[head],
                blocks[step, :, :HEAD_WIDTH],
                (((1,), (1,)), ((), ())),
                preferred_element_type=jnp.float32,
            )
            raised = jnp.where(seen, jnp.exp2(jnp.tanh(scores) * RAISE), 0.0)
            total[head] += jnp.dot(
                raised.astype(jnp.bfloat16), wide[...], preferred_element_type=jnp.float32
            )
        return carried

    lax.fori_loop(0, len(SLOTS), visit, 0)

    for mine in range(2):
        value = total[2 * other + mine]
        ready[:, mine * HEAD_WIDTH : (mine + 1) * HEAD_WIDTH] = (
            value[:, :HEAD_WIDTH] / value[:, HEAD_WIDTH:]
        ).astype(jnp.bfloat16)
    swap_back = start_copy(ready, landing, swap_s.at[2], swap_r.at[2], section=other)
    swap_back.start()
    for mine in range(2):
        value = total[2 * section + mine]
        out_ref[section, :, mine * HEAD_WIDTH : (mine + 1) * HEAD_WIDTH] = (
            value[:, :HEAD_WIDTH] / value[:, HEAD_WIDTH:]
        ).astype(jnp.bfloat16)
    swap_back.wait_recv()
    out_ref[other] = landing[...]
    swap_back.wait_send()
    swap_queries().wait_send()
    pl.when(section == 0)(lambda: hand_keys().wait_send())
    for step in range(4):
        climb(step).wait_send()
    for row in range(3):
        to_right(row).wait_send()
        to_left(row).wait_send()
        pass_keys(row).wait_send()
        pass_values(row).wait_send()
    edge_right(0).wait_send()
    edge_left(0).wait_send()
    edge_far(0).wait_send()


def attention(queries, own_kv, starts, meta):
    rows = starts.shape[0]
    dma = pltpu.SemaphoreType.DMA
    whole = pl.BlockSpec(memory_space=pltpu.VMEM)
    return pl.pallas_call(
        attention_kernel,
        out_shape=jax.ShapeDtypeStruct((2, rows, 2 * HEAD_WIDTH), jnp.bfloat16),
        in_specs=[pl.BlockSpec(memory_space=pltpu.SMEM), whole, whole, whole],
        out_specs=whole,
        scratch_shapes=[
            pltpu.VMEM((4, rows, HEAD_WIDTH), jnp.bfloat16),
            pltpu.VMEM((len(SLOTS), rows, 2 * HEAD_WIDTH), jnp.bfloat16),
            pltpu.VMEM((4, rows, 2 * HEAD_WIDTH), jnp.float32),
            pltpu.VMEM((rows, 2 * HEAD_WIDTH), jnp.bfloat16),
            pltpu.VMEM((rows, 2 * HEAD_WIDTH), jnp.bfloat16),
            pltpu.VMEM((rows, 2 * HEAD_WIDTH), jnp.bfloat16),
            dma((3,)), dma((3,)), dma((2,)),
            dma((4,)), dma((4,)), dma((4,)), dma((4,)), dma((4,)), dma((4,)),
            dma((3,)), dma((3,)), dma((3,)), dma((3,)), dma((1,)), dma((1,)),
        ],
        compiler_params=pltpu.CompilerParams(
            collective_id=1, has_side_effects=True, vmem_limit_bytes=56 * 2**20
        ),
        name="attention",
    )(meta, queries, own_kv, starts)


PIECES = 3


def mix_kernel(
    heads_ref, weight_hbm, hidden_ref, gain_ref, out_ref,
    weight, far_out, near_out, sum_out, far_in, near_in, sum_in, mixed,
    load, far_s, far_r, near_s, near_r, sum_s, sum_r,
):
    place = lax.axis_index("head")
    count = 4
    sides = ((place + 1) % count, (place + 3) % count)
    opposite = (place + 2) % count
    rows, width = mixed.shape
    half = width // 2
    piece = half // PIECES
    fetch = pltpu.make_async_copy(weight_hbm, weight, load.at[0])
    fetch.start()
    greet([{"head": sides[0]}, {"head": sides[1]}])
    fetch.wait()
    depth = heads_ref.shape[2]

    def partial(target, low):
        span = pl.ds(pl.multiple_of(target * rows, rows), rows)
        return jnp.dot(
            heads_ref[0, span, :], weight[:depth, low : low + piece], preferred_element_type=jnp.float32
        ) + jnp.dot(
            heads_ref[1, span, :], weight[depth:, low : low + piece], preferred_element_type=jnp.float32
        )

    def send(source, target, sent, landed, side, part):
        return start_copy(
            source.at[side, part], target.at[side, part], sent.at[side, part], landed.at[side, part],
            head=sides[side],
        )

    def far_copy(side, part):
        return send(far_out, far_in, far_s, far_r, side, part)

    def near_copy(side, part):
        return send(near_out, near_in, near_s, near_r, side, part)

    def sum_copy(side, part):
        return send(sum_out, sum_in, sum_s, sum_r, side, part)

    for part in range(PIECES):
        for side in range(2):
            low = side * half + part * piece
            far_out[side, part] = partial(opposite, low).astype(jnp.bfloat16)
            far_copy(side, part).start()
    for part in range(PIECES):
        for side in range(2):
            low = (1 - side) * half + part * piece
            near_out[side, part] = partial(sides[side], low).astype(jnp.bfloat16)
            near_copy(side, part).start()
    for part in range(PIECES):
        for side in range(2):
            low = side * half + part * piece
            own = partial(sides[side], low).astype(jnp.bfloat16).astype(jnp.float32)
            far_copy(side, part).wait_recv()
            sum_out[side, part] = (own + far_in[side, part].astype(jnp.float32)).astype(jnp.bfloat16)
            sum_copy(side, part).start()
    for part in range(2 * PIECES):
        low = part * piece
        mixed[:, low : low + piece] = partial(place, low).astype(jnp.bfloat16).astype(jnp.float32)
    for part in range(PIECES):
        for side in range(2):
            low = (1 - side) * half + part * piece
            near_copy(side, part).wait_recv()
            mixed[:, low : low + piece] += near_in[side, part].astype(jnp.float32)
    squares = jnp.zeros((rows, 128), jnp.float32)
    for part in range(PIECES):
        for side in range(2):
            low = side * half + part * piece
            sum_copy(side, part).wait_recv()
            value = mixed[:, low : low + piece] + sum_in[side, part].astype(jnp.float32)
            mixed[:, low : low + piece] = value
            square = value * value
            for column in range(0, piece, 128):
                squares = squares + square[:, column : column + 128]
    scale = lax.rsqrt(jnp.sum(squares, axis=-1, keepdims=True) / width + epsilon)
    for part in range(2 * PIECES):
        span = slice(part * piece, (part + 1) * piece)
        out_ref[:, span] = (
            hidden_ref[:, span].astype(jnp.float32) + mixed[:, span] * scale * gain_ref[:, span]
        ).astype(jnp.bfloat16)
    for part in range(PIECES):
        for side in range(2):
            far_copy(side, part).wait_send()
            near_copy(side, part).wait_send()
            sum_copy(side, part).wait_send()


def mix(heads, weight, hidden, gain):
    rows, width = hidden.shape
    dma = pltpu.SemaphoreType.DMA
    whole = pl.BlockSpec(memory_space=pltpu.VMEM)
    slots = pltpu.VMEM((2, PIECES, rows, width // (2 * PIECES)), jnp.bfloat16)
    return pl.pallas_call(
        mix_kernel,
        out_shape=jax.ShapeDtypeStruct((rows, width), jnp.bfloat16),
        in_specs=[whole, pl.BlockSpec(memory_space=pl.ANY), whole, whole],
        out_specs=whole,
        scratch_shapes=[
            pltpu.VMEM(weight.shape, jnp.bfloat16),
            slots, slots, slots, slots, slots, slots,
            pltpu.VMEM((rows, width), jnp.float32),
            dma((1,)),
        ]
        + [dma((2, PIECES))] * 6,
        compiler_params=pltpu.CompilerParams(
            collective_id=2, has_side_effects=True, vmem_limit_bytes=56 * 2**20
        ),
        name="mix",
    )(heads, weight, hidden, gain)


def project_kernel(
    hidden_ref, gain_ref, cos_ref, sin_ref, query_hbm, share_ref, q_out, kv_out,
    normed, query_weight, kv_weight,
    load, side_s, side_r, x_s, x_r, z_s, z_r,
):
    section = lax.axis_index("section")
    shard = lax.axis_index("seq")
    place = lax.axis_index("head")
    z, x = shard // XS, shard % XS
    up = ((z + 1) % ZS) * XS + x
    down = ((z + ZS - 1) % ZS) * XS + x
    rows, width = hidden_ref.shape
    half = width // 2
    piece = half // PIECES
    depth = share_ref.shape[0]
    sides = ((place + 1) % 4, (place + 3) % 4)
    across = [z * XS + (x + step) % XS for step in (1, 3, 2)]
    fetch = pltpu.make_async_copy(query_hbm, query_weight, load.at[0])
    fetch.start()
    greet([{"head": sides[0]}, {"head": sides[1]}] + [{"seq": seq} for seq in across + [up, down]])

    def weight_rows(zz, xx):
        return pl.ds(pl.multiple_of((zz * XS + xx) * depth, 16), depth)

    def share_across(number):
        return start_copy(
            share_ref, kv_weight.at[weight_rows(z, x)], x_s.at[number], x_r.at[number], seq=across[number]
        )

    def climb(side, hop, aside):
        back = hop - 1
        origin = (z + ZS - back) % ZS if side == 0 else (z + back) % ZS
        span = weight_rows(origin, (x + aside) % XS)
        source = share_ref if hop == 1 and aside == 0 else kv_weight.at[span]
        return start_copy(
            source, kv_weight.at[span], z_s.at[side, hop - 1, aside], z_r.at[side, hop - 1, aside],
            seq=(up, down)[side],
        )

    climbs = [
        (side, hop, aside)
        for hop in range(1, 5)
        for aside in range(4)
        for side in range(2)
        if hop < 4 or (aside < 2) == (side == 0)
    ]

    def row_copy(side, kind, part):
        which = side if kind == 0 else 1 - side
        span = pl.ds((side if kind == 2 else which) * half + part * piece, piece)
        source = (0, 0, 1 + side)[kind]
        target = (1 + side, 1 + side, 3)[kind]
        return start_copy(
            normed.at[source, :, span], normed.at[target, :, span],
            side_s.at[side, kind, part], side_r.at[side, kind, part], head=sides[side],
        )

    @pl.when(section == 0)
    def _():
        for number in range(3):
            share_across(number).start()
        for side in range(2):
            climb(side, 1, 0).start()
        kv_weight[weight_rows(z, x), :] = share_ref[...]

    squares = jnp.zeros((rows, 128), jnp.float32)
    for column in range(0, width, 128):
        value = hidden_ref[:, column : column + 128].astype(jnp.float32)
        squares = squares + value * value
    scale = lax.rsqrt(jnp.sum(squares, axis=-1, keepdims=True) / width + epsilon)
    for part in range(2 * PIECES):
        span = slice(part * piece, (part + 1) * piece)
        normed[0, :, span] = (
            hidden_ref[:, span].astype(jnp.float32) * scale * gain_ref[:, span]
        ).astype(jnp.bfloat16)
    for kind in range(2):
        for part in range(PIECES):
            for side in range(2):
                row_copy(side, kind, part).start()

    @pl.when(section == 0)
    def _():
        for number, aside in ((0, 3), (1, 1), (2, 2)):
            share_across(number).wait_recv()
            for side in range(2):
                climb(side, 1, aside).start()

    steps = (0, 3, 1, 2)

    def product(first, count, weight, low):
        return jnp.dot(
            normed[first : first + count].reshape(count * rows, width),
            weight[:, low : low + 2 * HEAD_WIDTH],
            preferred_element_type=jnp.float32,
        )

    def token_rows(slot):
        return pl.ds(pl.multiple_of(((place + steps[slot]) % 4) * rows, rows), rows)

    def turned(value, span):
        return value * cos_ref[span, :] + pltpu.roll(value, HEAD_WIDTH // 2, 1) * sin_ref[span, :]

    def make_queries(first, count):
        for pair in range(2):
            result = product(first, count, query_weight, pair * 2 * HEAD_WIDTH)
            for slot in range(count):
                span = token_rows(first + slot)
                for mine in range(2):
                    value = result[slot * rows : (slot + 1) * rows, mine * HEAD_WIDTH : (mine + 1) * HEAD_WIDTH]
                    q_out[2 * pair + mine, span, :] = (
                        turned(value, span) * (query_scale / softcap_limit)
                    ).astype(jnp.bfloat16)

    def make_keys(first, count):
        for pair in range(2):
            result = product(first, count, kv_weight, pair * 2 * HEAD_WIDTH)
            for slot in range(count):
                span = token_rows(first + slot)
                for mine in range(2):
                    value = result[slot * rows : (slot + 1) * rows, mine * HEAD_WIDTH : (mine + 1) * HEAD_WIDTH]
                    if pair == 0:
                        value = turned(value, span)
                    kv_out[mine, span, pair * HEAD_WIDTH : (pair + 1) * HEAD_WIDTH] = value.astype(jnp.bfloat16)

    def pass_weights(hop):
        @pl.when(section == 0)
        def _():
            for side, at, aside in climbs:
                if at == hop:
                    climb(side, hop, aside).wait_recv()
                    if (side, hop + 1, aside) in climbs:
                        climb(side, hop + 1, aside).start()

    fetch.wait()
    make_queries(0, 1)
    pass_weights(1)
    pass_weights(2)
    for part in range(PIECES):
        for side in range(2):
            row_copy(side, 0, part).wait_recv()
            row_copy(side, 2, part).start()
    pass_weights(3)
    for part in range(PIECES):
        for side in range(2):
            row_copy(side, 1, part).wait_recv()
    make_queries(1, 2)
    pass_weights(4)
    pl.when(section == 0)(lambda: make_keys(0, 3))
    for part in range(PIECES):
        for side in range(2):
            row_copy(side, 2, part).wait_recv()
    pl.when(section == 0)(lambda: make_keys(3, 1))
    make_queries(3, 1)
    for side in range(2):
        for kind in range(3):
            for part in range(PIECES):
                row_copy(side, kind, part).wait_send()

    @pl.when(section == 0)
    def _():
        for number in range(3):
            share_across(number).wait_send()
        for at in climbs:
            climb(*at).wait_send()


def project(hidden, gain, cosine, sine, query_weight, share):
    rows, width = hidden.shape
    tokens = cosine.shape[0]
    columns = query_weight.shape[1]
    dma = pltpu.SemaphoreType.DMA
    whole = pl.BlockSpec(memory_space=pltpu.VMEM)
    return pl.pallas_call(
        project_kernel,
        out_shape=(
            jax.ShapeDtypeStruct((4, tokens, HEAD_WIDTH), jnp.bfloat16),
            jax.ShapeDtypeStruct((2, tokens, 2 * HEAD_WIDTH), jnp.bfloat16),
        ),
        in_specs=[whole, whole, whole, whole, pl.BlockSpec(memory_space=pl.ANY), whole],
        out_specs=(whole, whole),
        scratch_shapes=[
            pltpu.VMEM((4, rows, width), jnp.bfloat16),
            pltpu.VMEM((width, columns), jnp.bfloat16),
            pltpu.VMEM((width, share.shape[1]), jnp.bfloat16),
            dma((1,)),
            dma((2, 3, PIECES)), dma((2, 3, PIECES)), dma((3,)), dma((3,)), dma((2, 4, 4)), dma((2, 4, 4)),
        ],
        compiler_params=pltpu.CompilerParams(
            collective_id=3, has_side_effects=True, vmem_limit_bytes=56 * 2**20
        ),
        name="project",
    )(hidden, gain, cosine, sine, query_weight, share)


def visits(shard, rows, block_table):
    z, x = shard // XS, shard % XS
    back = jnp.array([row for row, _ in SLOTS], jnp.int32)
    aside = jnp.array([column for _, column in SLOTS], jnp.int32)
    source = (x + XS - aside) % XS
    back = jnp.where(back < 0, jnp.where(source < x, 0, 4), back)
    block = (z - back) * XS + source
    listed = block_table[shard][jnp.maximum(block, 0)]
    return jnp.stack([block * rows, listed])


def local(hidden, q_weight, key_value_weight, o_weight, in_gain, post_gain, positions, block_table):
    shard = lax.axis_index("seq")
    tokens = 4 * hidden.shape[1]
    first = shard * tokens
    at = lax.dynamic_slice_in_dim(positions, first, tokens)
    lane = jnp.arange(HEAD_WIDTH, dtype=jnp.int32)
    frequency = 10000.0 ** (-((lane % (HEAD_WIDTH // 2)).astype(jnp.float32) * 2.0 / HEAD_WIDTH))
    angles = at.astype(jnp.float32)[:, None] * frequency[None, :]
    sine = jnp.sin(angles) * jnp.where(lane < HEAD_WIDTH // 2, -1.0, 1.0)
    share = key_value_weight.reshape(key_value_weight.shape[0], -1)
    queries, own_kv = project(hidden[0], in_gain, jnp.cos(angles), sine, q_weight[0], share)
    starts = jnp.broadcast_to(
        (first + jnp.arange(tokens, dtype=jnp.int32) - at)[:, None], (tokens, HEAD_WIDTH)
    )
    attended = attention(queries, own_kv, starts, visits(shard, tokens, block_table))
    return mix(attended, o_weight[0], hidden[0], post_gain)[None]


def solution(mesh):
    placed = (
        P("section", ("seq", "head"), None),
        P("section", None, "head"),
        P("seq", None, "head"),
        P("section", "head", None),
        P("section", None),
        P("section", None),
        P(),
        P(),
    )
    return jax.shard_map(
        local,
        mesh=mesh,
        in_specs=placed,
        out_specs=P("section", ("seq", "head"), None),
        check_vma=False,
    )
```

```python
import math

import functools

import jax
import jax.numpy as jnp
from jax import lax
from jax.experimental import pallas as pl
from jax.experimental.pallas import tpu as pltpu
from jax.sharding import PartitionSpec as P

HEAD_WIDTH = 128


epsilon = 1e-06
softcap_limit = 50.0
query_scale = 144.0 ** (-0.5)
RAISE = softcap_limit * math.log2(math.e)
XS, ZS = 4, 8


SLOTS = (
    (0, 0), (1, 0), (2, 0), (1, 1), (1, 3), (3, 0), (4, 0), (2, 1), (2, 3),
    (1, 2), (3, 1), (3, 3), (-1, 1), (-1, 3), (2, 2), (3, 2), (-1, 2),
)
PARTS = ((0, 384), (384, 128))
PIECES = 3


def start_copy(source, target, sent, landed, **place):
    copy = pltpu.make_async_remote_copy(
        src_ref=source,
        dst_ref=target,
        send_sem=sent,
        recv_sem=landed,
        device_id=place,
        device_id_type=pl.DeviceIdType.MESH,
    )
    return copy


def greet(places):
    barrier = pltpu.get_barrier_semaphore()
    for place in places:
        pl.semaphore_signal(
            barrier, inc=1, device_id=place, device_id_type=pl.DeviceIdType.MESH
        )
    pl.semaphore_wait(barrier, len(places))


def layer_kernel(
    table, hidden_ref, gain_ref, cos_ref, sin_ref, query_hbm, share_ref, start_ref, out_hbm, post_ref, out_ref,
    meta, normed, query_weight, kv_weight, out_weight, made_queries, made_kv, queries, blocks, starts,
    total, wide, ready, heads, far_out, near_out, sum_out, far_in, near_in, sum_in, mixed,
    load, side_s, side_r, x_s, x_r, w_s, w_r, swap_s, swap_r, own_s, hand_s, hand_r,
    z_s, z_r, right_s, right_r, left_s, left_r, key_s, key_r, value_s, value_r, edge_s, edge_r,
    far_s, far_r, near_s, near_r, sum_s, sum_r,
):
    section = lax.axis_index("section")
    shard = lax.axis_index("seq")
    place = lax.axis_index("head")
    other = 1 - section
    z, x = shard // XS, shard % XS
    up = ((z + 1) % ZS) * XS + x
    down = ((z + ZS - 1) % ZS) * XS + x
    across = [z * XS + (x + step) % XS for step in (1, 3, 2)]
    right, left = across[0], across[1]
    rows, width = hidden_ref.shape
    tokens = start_ref.shape[0]
    half = width // 2
    piece = half // PIECES
    depth = share_ref.shape[0]
    sides = ((place + 1) % 4, (place + 3) % 4)
    steps = (0, 3, 1, 2)
    fetch = pltpu.make_async_copy(query_hbm, query_weight, load.at[0])
    fetch.start()
    fetch_out = pltpu.make_async_copy(out_hbm, out_weight, load.at[1])
    greet(
        [{"head": sides[0]}, {"head": sides[1]}, {"section": other}]
        + [{"seq": seq} for seq in across + [up, down]]
    )

    def weight_rows(zz, xx):
        return pl.ds(pl.multiple_of((zz * XS + xx) * depth, 16), depth)

    def share_across(number):
        return start_copy(
            share_ref, kv_weight.at[weight_rows(z, x)], x_s.at[number], x_r.at[number], seq=across[number]
        )

    def climb_weights(side, hop, aside):
        back = hop - 1
        origin = (z + ZS - back) % ZS if side == 0 else (z + back) % ZS
        span = weight_rows(origin, (x + aside) % XS)
        source = share_ref if hop == 1 and aside == 0 else kv_weight.at[span]
        return start_copy(
            source, kv_weight.at[span], w_s.at[side, hop - 1, aside], w_r.at[side, hop - 1, aside],
            seq=(up, down)[side],
        )

    climbs = [
        (side, hop, aside)
        for hop in range(1, 5)
        for aside in range(4)
        for side in range(2)
        if hop < 4 or (aside < 2) == (side == 0)
    ]

    def row_copy(side, kind, part):
        which = side if kind == 0 else 1 - side
        span = pl.ds((side if kind == 2 else which) * half + part * piece, piece)
        source = (0, 0, 1 + side)[kind]
        target = (1 + side, 1 + side, 3)[kind]
        return start_copy(
            normed.at[source, :, span], normed.at[target, :, span],
            side_s.at[side, kind, part], side_r.at[side, kind, part], head=sides[side],
        )

    def token_rows(slot):
        return pl.ds(pl.multiple_of(((place + steps[slot]) % 4) * rows, rows), rows)

    @pl.when(section == 0)
    def _():
        for number in range(3):
            share_across(number).start()
        for side in range(2):
            climb_weights(side, 1, 0).start()
        kv_weight[weight_rows(z, x), :] = share_ref[...]

    squares = jnp.zeros((rows, 128), jnp.float32)
    for column in range(0, width, 128):
        value = hidden_ref[:, column : column + 128].astype(jnp.float32)
        squares = squares + value * value
    scale = lax.rsqrt(jnp.sum(squares, axis=-1, keepdims=True) / width + epsilon)
    for part in range(2 * PIECES):
        span = slice(part * piece, (part + 1) * piece)
        normed[0, :, span] = (
            hidden_ref[:, span].astype(jnp.float32) * scale * gain_ref[:, span]
        ).astype(jnp.bfloat16)
    for kind in range(2):
        for part in range(PIECES):
            for side in range(2):
                row_copy(side, kind, part).start()

    @pl.when(section == 0)
    def _():
        for number, aside in ((0, 3), (1, 1), (2, 2)):
            share_across(number).wait_recv()
            for side in range(2):
                climb_weights(side, 1, aside).start()

    for number, (back, aside) in enumerate(SLOTS):
        source = (x + XS - aside) % XS
        row = jnp.where(source < x, 0, 4) if back < 0 else back
        block = (z - row) * XS + source
        meta[0, number] = block * tokens
        meta[1, number] = table[shard, jnp.maximum(block, 0)]
    for slot in range(4):
        starts[slot * rows : (slot + 1) * rows, :] = start_ref[token_rows(slot), :]
    total[...] = jnp.zeros_like(total)
    wide[...] = jnp.ones_like(wide)

    def product(first, count, weight, low):
        return jnp.dot(
            normed[first : first + count].reshape(count * rows, width),
            weight[:, low : low + 2 * HEAD_WIDTH],
            preferred_element_type=jnp.float32,
        )

    def turned(value, span):
        return value * cos_ref[span, :] + pltpu.roll(value, HEAD_WIDTH // 2, 1) * sin_ref[span, :]

    def make_queries(first, count):
        for pair in range(2):
            result = product(first, count, query_weight, pair * 2 * HEAD_WIDTH)
            for slot in range(count):
                low = (first + slot) * rows
                for mine in range(2):
                    value = result[slot * rows : (slot + 1) * rows, mine * HEAD_WIDTH : (mine + 1) * HEAD_WIDTH]
                    made_queries[2 * pair + mine, low : low + rows, :] = (
                        turned(value, token_rows(first + slot)) * (query_scale / softcap_limit)
                    ).astype(jnp.bfloat16)

    def make_keys(first, count):
        for pair in range(2):
            result = product(first, count, kv_weight, pair * 2 * HEAD_WIDTH)
            for slot in range(count):
                low = (first + slot) * rows
                for mine in range(2):
                    value = result[slot * rows : (slot + 1) * rows, mine * HEAD_WIDTH : (mine + 1) * HEAD_WIDTH]
                    if pair == 0:
                        value = turned(value, token_rows(first + slot))
                    made_kv[mine, low : low + rows, pair * HEAD_WIDTH : (pair + 1) * HEAD_WIDTH] = value.astype(
                        jnp.bfloat16
                    )

    def pass_weights(hop):
        @pl.when(section == 0)
        def _():
            for side, at, aside in climbs:
                if at == hop:
                    climb_weights(side, hop, aside).wait_recv()
                    if (side, hop + 1, aside) in climbs:
                        climb_weights(side, hop + 1, aside).start()

    def span_of(part):
        return pl.ds(*PARTS[part])

    def hand_keys(part):
        span = span_of(part)
        return start_copy(
            made_kv.at[1, span], blocks.at[0, span], hand_s.at[part], hand_r.at[part], section=other
        )

    def own_keys(part):
        span = span_of(part)
        return pltpu.make_async_copy(made_kv.at[0, span], blocks.at[0, span], own_s.at[1 + part])

    def block_copy(source, target, part, sent, landed, seq, columns=(0, 2 * HEAD_WIDTH)):
        span, width_of = span_of(part), pl.ds(*columns)
        return start_copy(
            blocks.at[source, span, width_of], blocks.at[target, span, width_of], sent, landed, seq=seq
        )

    def climb(step, part):
        slots = (0, 1, 2, 5, 6)
        return block_copy(slots[step], slots[step + 1], part, z_s.at[step, part], z_r.at[step, part], up)

    def to_right(row, part):
        source, target = ((1, 3), (2, 7), (5, 10))[row]
        return block_copy(source, target, part, right_s.at[row, part], right_r.at[row, part], right)

    def to_left(row, part):
        source, target = ((1, 4), (2, 8), (5, 11))[row]
        return block_copy(source, target, part, left_s.at[row, part], left_r.at[row, part], left)

    keys_of, values_of = (0, HEAD_WIDTH), (HEAD_WIDTH, HEAD_WIDTH)

    def pass_keys(row, part):
        source, target = ((3, 9), (7, 14), (10, 15))[row]
        return block_copy(source, target, part, key_s.at[row, part], key_r.at[row, part], right, keys_of)

    def pass_values(row, part):
        source, target = ((4, 9), (8, 14), (11, 15))[row]
        return block_copy(source, target, part, value_s.at[row, part], value_r.at[row, part], left, values_of)

    def edge_right(source, part):
        return block_copy(source, 12, part, right_s.at[3, part], right_r.at[3, part], right)

    def edge_left(source, part):
        return block_copy(source, 13, part, left_s.at[3, part], left_r.at[3, part], left)

    def edge_far(kind, part):
        return block_copy(
            (12, 12, 13, 13)[kind], 16, part, edge_s.at[kind, part], edge_r.at[kind % 2, part],
            (right, right, left, left)[kind], (keys_of, values_of)[kind % 2],
        )

    far_when = (x < 3, x == 2, x == 1, x > 0)

    def begin(part):
        climb(0, part).start()
        pl.when(x < 3)(lambda: edge_right(0, part).start())
        pl.when(x == 0)(lambda: edge_left(0, part).start())

    def climbed(step, part):
        climb(step, part).wait_recv()
        if step < 3:
            climb(step + 1, part).start()
            to_right(step, part).start()
            to_left(step, part).start()
        else:
            pl.when(x == 3)(lambda: edge_right(6, part).start())
            pl.when(x > 0)(lambda: edge_left(6, part).start())

    def spread(row, part):
        to_right(row, part).wait_recv()
        pass_keys(row, part).start()
        to_left(row, part).wait_recv()
        pass_values(row, part).start()

    def passed(row):
        for part in range(2):
            pass_keys(row, part).wait_recv()
            pass_values(row, part).wait_recv()

    def got_right():
        for part in range(2):
            edge_right(0, part).wait_recv()
            for kind in (0, 1):
                pl.when(far_when[kind])(edge_far(kind, part).start)

    def got_left():
        for part in range(2):
            edge_left(0, part).wait_recv()
            for kind in (2, 3):
                pl.when(far_when[kind])(edge_far(kind, part).start)

    fetch.wait()
    make_queries(0, 1)
    pass_weights(1)
    pass_weights(2)
    for part in range(PIECES):
        for side in range(2):
            row_copy(side, 0, part).wait_recv()
            row_copy(side, 2, part).start()
    pass_weights(3)
    for part in range(PIECES):
        for side in range(2):
            row_copy(side, 1, part).wait_recv()
    pass_weights(4)

    @pl.when(section == 0)
    def _():
        make_keys(0, 3)
        hand_keys(0).start()
        own_keys(0).start()
        own_keys(0).wait()

    @pl.when(section == 1)
    def _():
        make_queries(1, 2)
        hand_keys(0).wait_recv()

    begin(0)
    pl.when(section == 0)(lambda: make_queries(1, 2))
    fetch_out.start()
    climbed(0, 0)
    for part in range(PIECES):
        for side in range(2):
            row_copy(side, 2, part).wait_recv()

    @pl.when(section == 0)
    def _():
        make_keys(3, 1)
        hand_keys(1).start()
        own_keys(1).start()
        own_keys(1).wait()

    pl.when(section == 1)(lambda: hand_keys(1).wait_recv())
    begin(1)
    make_queries(3, 1)
    swap_queries = start_copy(
        made_queries.at[pl.ds(2 * other, 2)], queries.at[pl.ds(2 * section, 2)],
        swap_s.at[0], swap_r.at[0], section=other,
    )
    own_queries = pltpu.make_async_copy(
        made_queries.at[pl.ds(2 * section, 2)], queries.at[pl.ds(2 * section, 2)], own_s.at[0]
    )
    swap_queries.start()
    own_queries.start()
    spread(0, 0)
    climbed(1, 0)
    own_queries.wait()
    swap_queries.wait_recv()

    def token_of(index):
        slot = index // rows
        base = jnp.zeros_like(index)
        for number in range(4):
            base = jnp.where(slot == number, ((place + steps[number]) % 4) * rows, base)
        return base + index % rows

    key_token = token_of(lax.broadcasted_iota(jnp.int32, (1, tokens), 1))
    query_token = shard * tokens + token_of(lax.broadcasted_iota(jnp.int32, (tokens, 1), 0))

    def turn(step):
        if step == 1:
            climbed(0, 1)
        elif step == 2:
            climbed(2, 0)
            climbed(1, 1)
            pl.when(x > 0)(got_right)
            pl.when(x == 3)(got_left)
        elif step == 3:
            spread(1, 0)
            spread(0, 1)
        elif step == 5:
            climbed(3, 0)
            climbed(2, 1)
        elif step == 6:
            spread(2, 0)
            climbed(3, 1)
        elif step == 7:
            spread(1, 1)
        elif step == 9:
            passed(0)
        elif step == 10:
            spread(2, 1)
        elif step == 12:
            pl.when(x == 0)(got_right)
            pl.when(x < 3)(got_left)
        elif step == 14:
            passed(1)
        elif step == 15:
            passed(2)
        elif step == 16:
            for part in range(2):
                for kind in range(2):
                    edge_far(kind, part).wait_recv()

    def visit(step, carried):
        for number in (1, 2, 3, 5, 6, 7, 9, 10, 12, 14, 15, 16):
            pl.when(step == number)(functools.partial(turn, number))
        keys = meta[0, step] + key_token
        listed = meta[1, step] == 1
        start = jnp.where(listed, starts[:, :1], shard * tokens + tokens)
        seen = (keys >= start) & (keys <= query_token)
        wide[:, :HEAD_WIDTH] = blocks[step, :, HEAD_WIDTH:]
        for head in range(4):
            scores = lax.dot_general(
                queries[head],
                blocks[step, :, :HEAD_WIDTH],
                (((1,), (1,)), ((), ())),
                preferred_element_type=jnp.float32,
            )
            raised = jnp.where(seen, jnp.exp2(jnp.tanh(scores) * RAISE), 0.0)
            total[head] += jnp.dot(
                raised.astype(jnp.bfloat16), wide[...], preferred_element_type=jnp.float32
            )
        return carried

    lax.fori_loop(0, len(SLOTS), visit, 0)

    for mine in range(2):
        value = total[2 * other + mine]
        ready[:, mine * HEAD_WIDTH : (mine + 1) * HEAD_WIDTH] = (
            value[:, :HEAD_WIDTH] / value[:, HEAD_WIDTH:]
        ).astype(jnp.bfloat16)
    swap_back = start_copy(ready, heads.at[section], swap_s.at[1], swap_r.at[1], section=other)
    swap_back.start()
    for mine in range(2):
        value = total[2 * section + mine]
        heads[section, :, mine * HEAD_WIDTH : (mine + 1) * HEAD_WIDTH] = (
            value[:, :HEAD_WIDTH] / value[:, HEAD_WIDTH:]
        ).astype(jnp.bfloat16)
    fetch_out.wait()
    swap_back.wait_recv()

    near_slot = (2, 1)
    inner = 2 * HEAD_WIDTH

    def partial(slot, low):
        span = slice(slot * rows, (slot + 1) * rows)
        return jnp.dot(
            heads[0, span, :], out_weight[:inner, low : low + piece], preferred_element_type=jnp.float32
        ) + jnp.dot(
            heads[1, span, :], out_weight[inner:, low : low + piece], preferred_element_type=jnp.float32
        )

    def send(source, target, sent, landed, side, part):
        return start_copy(
            source.at[side, part], target.at[side, part], sent.at[side, part], landed.at[side, part],
            head=sides[side],
        )

    def far_copy(side, part):
        return send(far_out, far_in, far_s, far_r, side, part)

    def near_copy(side, part):
        return send(near_out, near_in, near_s, near_r, side, part)

    def sum_copy(side, part):
        return send(sum_out, sum_in, sum_s, sum_r, side, part)

    for part in range(PIECES):
        for side in range(2):
            far_out[side, part] = partial(3, side * half + part * piece).astype(jnp.bfloat16)
            far_copy(side, part).start()
    for part in range(PIECES):
        for side in range(2):
            low = (1 - side) * half + part * piece
            near_out[side, part] = partial(near_slot[side], low).astype(jnp.bfloat16)
            near_copy(side, part).start()
    for part in range(PIECES):
        for side in range(2):
            low = side * half + part * piece
            own = partial(near_slot[side], low).astype(jnp.bfloat16).astype(jnp.float32)
            far_copy(side, part).wait_recv()
            sum_out[side, part] = (own + far_in[side, part].astype(jnp.float32)).astype(jnp.bfloat16)
            sum_copy(side, part).start()
    for part in range(2 * PIECES):
        low = part * piece
        mixed[:, low : low + piece] = partial(0, low).astype(jnp.bfloat16).astype(jnp.float32)
    for part in range(PIECES):
        for side in range(2):
            low = (1 - side) * half + part * piece
            near_copy(side, part).wait_recv()
            mixed[:, low : low + piece] += near_in[side, part].astype(jnp.float32)
    squares = jnp.zeros((rows, 128), jnp.float32)
    for part in range(PIECES):
        for side in range(2):
            low = side * half + part * piece
            sum_copy(side, part).wait_recv()
            value = mixed[:, low : low + piece] + sum_in[side, part].astype(jnp.float32)
            mixed[:, low : low + piece] = value
            square = value * value
            for column in range(0, piece, 128):
                squares = squares + square[:, column : column + 128]
    scale = lax.rsqrt(jnp.sum(squares, axis=-1, keepdims=True) / width + epsilon)
    for part in range(2 * PIECES):
        span = slice(part * piece, (part + 1) * piece)
        out_ref[:, span] = (
            hidden_ref[:, span].astype(jnp.float32) + mixed[:, span] * scale * post_ref[:, span]
        ).astype(jnp.bfloat16)

    for side in range(2):
        for part in range(PIECES):
            for kind in range(3):
                row_copy(side, kind, part).wait_send()
            far_copy(side, part).wait_send()
            near_copy(side, part).wait_send()
            sum_copy(side, part).wait_send()
    swap_back.wait_send()
    swap_queries.wait_send()
    for part in range(2):
        for step in range(4):
            climb(step, part).wait_send()
        for row in range(3):
            to_right(row, part).wait_send()
            to_left(row, part).wait_send()
            pass_keys(row, part).wait_send()
            pass_values(row, part).wait_send()
        edge_right(0, part).wait_send()
        edge_left(0, part).wait_send()
        for kind in range(4):
            pl.when(far_when[kind])(edge_far(kind, part).wait_send)

    @pl.when(section == 0)
    def _():
        for part in range(2):
            hand_keys(part).wait_send()
        for number in range(3):
            share_across(number).wait_send()
        for at in climbs:
            climb_weights(*at).wait_send()


def layer(table, hidden, gain, cosine, sine, query_weight, share, starts, out_weight, post_gain):
    rows, width = hidden.shape
    tokens = starts.shape[0]
    dma = pltpu.SemaphoreType.DMA
    whole = pl.BlockSpec(memory_space=pltpu.VMEM)
    apart = pl.BlockSpec(memory_space=pl.ANY)
    small = pl.BlockSpec(memory_space=pltpu.SMEM)
    pieces = pltpu.VMEM((2, PIECES, rows, width // (2 * PIECES)), jnp.bfloat16)

    def half_type(*shape):
        return pltpu.VMEM(shape, jnp.bfloat16)

    pair = 2 * HEAD_WIDTH
    return pl.pallas_call(
        layer_kernel,
        out_shape=jax.ShapeDtypeStruct((rows, width), jnp.bfloat16),
        in_specs=[small, whole, whole, whole, whole, apart, whole, whole, apart, whole],
        out_specs=whole,
        scratch_shapes=[
            pltpu.SMEM((2, len(SLOTS)), jnp.int32),
            half_type(4, rows, width),
            half_type(*query_weight.shape),
            half_type(width, share.shape[1]),
            half_type(*out_weight.shape),
            half_type(4, tokens, HEAD_WIDTH),
            half_type(2, tokens, pair),
            half_type(4, tokens, HEAD_WIDTH),
            half_type(len(SLOTS), tokens, pair),
            pltpu.VMEM((tokens, HEAD_WIDTH), jnp.int32),
            pltpu.VMEM((4, tokens, pair), jnp.float32),
            half_type(tokens, pair),
            half_type(tokens, pair),
            half_type(2, tokens, pair),
            pieces, pieces, pieces, pieces, pieces, pieces,
            pltpu.VMEM((rows, width), jnp.float32),
            dma((2,)), dma((2, 3, PIECES)), dma((2, 3, PIECES)), dma((3,)), dma((3,)),
            dma((2, 4, 4)), dma((2, 4, 4)), dma((2,)), dma((2,)), dma((3,)), dma((2,)), dma((2,)),
            dma((4, 2)), dma((4, 2)), dma((4, 2)), dma((4, 2)), dma((4, 2)), dma((4, 2)),
            dma((3, 2)), dma((3, 2)), dma((3, 2)), dma((3, 2)), dma((4, 2)), dma((2, 2)),
        ]
        + [dma((2, PIECES))] * 6,
        compiler_params=pltpu.CompilerParams(
            collective_id=1, has_side_effects=True, vmem_limit_bytes=62 * 2**20
        ),
        name="layer",
    )(table, hidden, gain, cosine, sine, query_weight, share, starts, out_weight, post_gain)


def local(hidden, q_weight, key_value_weight, o_weight, in_gain, post_gain, positions, block_table):
    shard = lax.axis_index("seq")
    tokens = 4 * hidden.shape[1]
    first = shard * tokens
    at = lax.dynamic_slice_in_dim(positions, first, tokens)
    lane = jnp.arange(HEAD_WIDTH, dtype=jnp.int32)
    frequency = 10000.0 ** (-((lane % (HEAD_WIDTH // 2)).astype(jnp.float32) * 2.0 / HEAD_WIDTH))
    angles = at.astype(jnp.float32)[:, None] * frequency[None, :]
    sine = jnp.sin(angles) * jnp.where(lane < HEAD_WIDTH // 2, -1.0, 1.0)
    share = key_value_weight.reshape(key_value_weight.shape[0], -1)
    starts = jnp.broadcast_to(
        (first + jnp.arange(tokens, dtype=jnp.int32) - at)[:, None], (tokens, HEAD_WIDTH)
    )
    return layer(
        block_table, hidden[0], in_gain, jnp.cos(angles), sine, q_weight[0], share, starts, o_weight[0], post_gain
    )[None]


def solution(mesh):
    placed = (
        P("section", ("seq", "head"), None),
        P("section", None, "head"),
        P("seq", None, "head"),
        P("section", "head", None),
        P("section", None),
        P("section", None),
        P(),
        P(),
    )
    return jax.shard_map(
        local,
        mesh=mesh,
        in_specs=placed,
        out_specs=P("section", ("seq", "head"), None),
        check_vma=False,
    )
```

```python
import math

import functools

import jax
import jax.numpy as jnp
from jax import lax
from jax.experimental import pallas as pl
from jax.experimental.pallas import tpu as pltpu
from jax.sharding import PartitionSpec as P

HEAD_WIDTH = 128


epsilon = 1e-06
softcap_limit = 50.0
query_scale = 144.0 ** (-0.5)
RAISE = softcap_limit * math.log2(math.e)
XS, ZS = 4, 8


SLOTS = (
    (0, 0), (1, 0), (2, 0), (1, 1), (1, 3), (3, 0), (4, 0), (2, 1), (2, 3),
    (1, 2), (3, 1), (3, 3), (-1, 1), (-1, 3), (2, 2), (3, 2), (-1, 2),
)
PARTS = ((0, 128), (128, 256), (384, 128))
BACK = ((384, 128), (0, 384))
FIRST = 64
PIECES = 3


def start_copy(source, target, sent, landed, **place):
    copy = pltpu.make_async_remote_copy(
        src_ref=source,
        dst_ref=target,
        send_sem=sent,
        recv_sem=landed,
        device_id=place,
        device_id_type=pl.DeviceIdType.MESH,
    )
    return copy


def greet(places):
    barrier = pltpu.get_barrier_semaphore()
    for place in places:
        pl.semaphore_signal(
            barrier, inc=1, device_id=place, device_id_type=pl.DeviceIdType.MESH
        )
    pl.semaphore_wait(barrier, len(places))


def layer_kernel(
    table, hidden_ref, gain_ref, position_ref, frequency_ref, query_hbm, share_ref, out_hbm, post_ref, out_ref,
    meta, normed, query_weight, kv_weight, out_weight, made_queries, made_kv, queries, blocks, starts, cosine, sine,
    total, wide, ready, heads, far_out, near_out, sum_out, far_in, near_in, sum_in, mixed,
    load, side_s, side_r, x_s, x_r, w_s, w_r, b_s, b_r, c_s, c_r, d_s, d_r, swap_s, swap_r, own_s, hand_s, hand_r,
    z_s, z_r, right_s, right_r, left_s, left_r, key_s, key_r, value_s, value_r, edge_s, edge_r,
    far_s, far_r, near_s, near_r, sum_s, sum_r,
):
    section = lax.axis_index("section")
    shard = lax.axis_index("seq")
    place = lax.axis_index("head")
    other = 1 - section
    z, x = shard // XS, shard % XS
    up = ((z + 1) % ZS) * XS + x
    down = ((z + ZS - 1) % ZS) * XS + x
    across = [z * XS + (x + step) % XS for step in (1, 3, 2)]
    right, left = across[0], across[1]
    rows, width = hidden_ref.shape
    tokens = 4 * rows
    half = width // 2
    piece = half // PIECES
    depth = share_ref.shape[0]
    sides = ((place + 1) % 4, (place + 3) % 4)
    steps = (0, 3, 1, 2)
    fetch = pltpu.make_async_copy(query_hbm, query_weight, load.at[0])
    fetch.start()
    fetch_out = pltpu.make_async_copy(out_hbm, out_weight, load.at[1])
    own_share = pl.ds(pl.multiple_of(shard * depth, 16), depth)
    columns = share_ref.shape[2]
    for number in range(2):
        kv_weight[own_share, number * columns : (number + 1) * columns] = share_ref[:, number, :]
    greet(
        [{"head": sides[0]}, {"head": sides[1]}, {"section": other}]
        + [{"seq": seq} for seq in across + [up, down]]
    )

    def weight_rows(zz, xx, second):
        low = (zz * XS + xx) * depth + (FIRST if second else 0)
        return pl.ds(pl.multiple_of(low, 16), depth - FIRST if second else FIRST)

    def weight_copy(zz, xx, second, sent, landed, seq):
        span = weight_rows(zz % ZS, xx % XS, second)
        return start_copy(kv_weight.at[span], kv_weight.at[span], sent, landed, seq=seq)

    def share_across(number):
        return weight_copy(z, x, False, x_s.at[number], x_r.at[number], across[number])

    def climb_weights(side, hop, aside):
        origin = z + ZS - (hop - 1) if side == 0 else z + (hop - 1)
        return weight_copy(
            origin, x + aside, False, w_s.at[side, hop - 1, aside], w_r.at[side, hop - 1, aside], (up, down)[side]
        )

    climbs = [
        (side, hop, aside)
        for hop in range(1, 5)
        for aside in range(4)
        for side in range(2)
        if hop < 4 or (aside < 2) == (side == 0)
    ]

    def climb_second(side, hop):
        origin = z + ZS - (hop - 1) if side == 0 else z + (hop - 1)
        return weight_copy(origin, x, True, b_s.at[side, hop - 1], b_r.at[side, hop - 1], (up, down)[side])

    second_climbs = [(side, hop) for hop in range(1, 5) for side in range(2) if hop < 4 or side == 0]

    def cross_second(side, back):
        return weight_copy(
            z + ZS - back, x, True, c_s.at[side, back], c_r.at[side, back], (right, left)[side]
        )

    def relay_second(back):
        side = back % 2
        return weight_copy(
            z + ZS - back, x + (3, 1)[side], True, d_s.at[back], d_r.at[back], (right, left)[side]
        )

    def row_copy(side, kind, part):
        which = side if kind == 0 else 1 - side
        span = pl.ds((side if kind == 2 else which) * half + part * piece, piece)
        source = (0, 0, 1 + side)[kind]
        target = (1 + side, 1 + side, 3)[kind]
        return start_copy(
            normed.at[source, :, span], normed.at[target, :, span],
            side_s.at[side, kind, part], side_r.at[side, kind, part], head=sides[side],
        )

    @pl.when(section == 0)
    def _():
        for number in range(3):
            share_across(number).start()
        for side in range(2):
            climb_second(side, 1).start()
            climb_weights(side, 1, 0).start()
            cross_second(side, 0).start()

    squares = jnp.zeros((rows, 128), jnp.float32)
    for column in range(0, width, 128):
        value = hidden_ref[:, column : column + 128].astype(jnp.float32)
        squares = squares + value * value
    scale = lax.rsqrt(jnp.sum(squares, axis=-1, keepdims=True) / width + epsilon)
    for part in range(2 * PIECES):
        span = slice(part * piece, (part + 1) * piece)
        normed[0, :, span] = (
            hidden_ref[:, span].astype(jnp.float32) * scale * gain_ref[:, span]
        ).astype(jnp.bfloat16)
    for kind in range(2):
        for part in range(PIECES):
            for side in range(2):
                row_copy(side, kind, part).start()

    @pl.when(section == 0)
    def _():
        for number, aside in ((0, 3), (1, 1), (2, 2)):
            share_across(number).wait_recv()
            for side in range(2):
                climb_weights(side, 1, aside).start()

    for number, (back, aside) in enumerate(SLOTS):
        source = (x + XS - aside) % XS
        row = jnp.where(source < x, 0, 4) if back < 0 else back
        block = (z - row) * XS + source
        meta[0, number] = block * tokens
        meta[1, number] = table[shard, jnp.maximum(block, 0)]
    lane = lax.broadcasted_iota(jnp.int32, (rows, HEAD_WIDTH), 1)
    line = lax.broadcasted_iota(jnp.int32, (rows, HEAD_WIDTH), 0)
    for slot in range(4):
        origin = (place + steps[slot]) % 4
        span = slice(slot * rows, (slot + 1) * rows)
        at = jnp.transpose(jnp.broadcast_to(position_ref[pl.ds(4 * shard + origin, 1), :], (rows, rows)))
        starts[span, :] = shard * tokens + origin * rows + line - at
        angle = at.astype(jnp.float32) * frequency_ref[...]
        cosine[span, :] = jnp.cos(angle)
        sine[span, :] = jnp.sin(angle) * jnp.where(lane < HEAD_WIDTH // 2, -1.0, 1.0)
    total[...] = jnp.zeros_like(total)
    wide[...] = jnp.ones_like(wide)

    def product(first, count, weight, low):
        return jnp.dot(
            normed[first : first + count].reshape(count * rows, width),
            weight[:, low : low + 2 * HEAD_WIDTH],
            preferred_element_type=jnp.float32,
        )

    def turned(value, span):
        return value * cosine[span, :] + pltpu.roll(value, HEAD_WIDTH // 2, 1) * sine[span, :]

    def make_queries(first, count):
        for pair in range(2):
            result = product(first, count, query_weight, pair * 2 * HEAD_WIDTH)
            for slot in range(count):
                low = (first + slot) * rows
                for mine in range(2):
                    value = result[slot * rows : (slot + 1) * rows, mine * HEAD_WIDTH : (mine + 1) * HEAD_WIDTH]
                    made_queries[2 * pair + mine, low : low + rows, :] = (
                        turned(value, slice(low, low + rows)) * (query_scale / softcap_limit)
                    ).astype(jnp.bfloat16)

    def make_keys(first, count):
        for pair in range(2):
            result = product(first, count, kv_weight, pair * 2 * HEAD_WIDTH)
            for slot in range(count):
                low = (first + slot) * rows
                for mine in range(2):
                    value = result[slot * rows : (slot + 1) * rows, mine * HEAD_WIDTH : (mine + 1) * HEAD_WIDTH]
                    if pair == 0:
                        value = turned(value, slice(low, low + rows))
                    made_kv[mine, low : low + rows, pair * HEAD_WIDTH : (pair + 1) * HEAD_WIDTH] = value.astype(
                        jnp.bfloat16
                    )

    def pass_weights(hop):
        @pl.when(section == 0)
        def _():
            for side, at in second_climbs:
                if at == hop:
                    climb_second(side, hop).wait_recv()
                    if (side, hop + 1) in second_climbs:
                        climb_second(side, hop + 1).start()
                    for across_side in range(2):
                        cross_second(across_side, hop if side == 0 else ZS - hop).start()
            for side, at, aside in climbs:
                if at == hop:
                    climb_weights(side, hop, aside).wait_recv()
                    if (side, hop + 1, aside) in climbs:
                        climb_weights(side, hop + 1, aside).start()
            for back in ((0,), (1, 7), (2, 6), (3, 5), (4,))[hop - 1]:
                for side in range(2):
                    cross_second(side, back).wait_recv()
                relay_second(back).start()

    def finish_weights():
        for side in range(2):
            cross_second(side, 4).wait_recv()
        relay_second(4).start()
        for back in range(ZS):
            relay_second(back).wait_recv()

    def span_of(part):
        return pl.ds(*PARTS[part])

    def hand_keys(part):
        span = span_of(part)
        return start_copy(
            made_kv.at[1, span], blocks.at[0, span], hand_s.at[part], hand_r.at[part], section=other
        )

    def own_keys(part):
        span = span_of(part)
        return pltpu.make_async_copy(made_kv.at[0, span], blocks.at[0, span], own_s.at[1 + part])

    def block_copy(source, target, part, sent, landed, seq, columns=(0, 2 * HEAD_WIDTH)):
        span, width_of = span_of(part), pl.ds(*columns)
        return start_copy(
            blocks.at[source, span, width_of], blocks.at[target, span, width_of], sent, landed, seq=seq
        )

    def climb(step, part):
        slots = (0, 1, 2, 5, 6)
        return block_copy(slots[step], slots[step + 1], part, z_s.at[step, part], z_r.at[step, part], up)

    def to_right(row, part):
        source, target = ((1, 3), (2, 7), (5, 10))[row]
        return block_copy(source, target, part, right_s.at[row, part], right_r.at[row, part], right)

    def to_left(row, part):
        source, target = ((1, 4), (2, 8), (5, 11))[row]
        return block_copy(source, target, part, left_s.at[row, part], left_r.at[row, part], left)

    keys_of, values_of = (0, HEAD_WIDTH), (HEAD_WIDTH, HEAD_WIDTH)

    def pass_keys(row, part):
        source, target = ((3, 9), (7, 14), (10, 15))[row]
        return block_copy(source, target, part, key_s.at[row, part], key_r.at[row, part], right, keys_of)

    def pass_values(row, part):
        source, target = ((4, 9), (8, 14), (11, 15))[row]
        return block_copy(source, target, part, value_s.at[row, part], value_r.at[row, part], left, values_of)

    def edge_right(source, part):
        return block_copy(source, 12, part, right_s.at[3, part], right_r.at[3, part], right)

    def edge_left(source, part):
        return block_copy(source, 13, part, left_s.at[3, part], left_r.at[3, part], left)

    def edge_far(kind, part):
        return block_copy(
            (12, 12, 13, 13)[kind], 16, part, edge_s.at[kind, part], edge_r.at[kind % 2, part],
            (right, right, left, left)[kind], (keys_of, values_of)[kind % 2],
        )

    far_when = (x < 3, x == 2, x == 1, x > 0)

    def begin(part):
        climb(0, part).start()
        pl.when(x < 3)(lambda: edge_right(0, part).start())
        pl.when(x == 0)(lambda: edge_left(0, part).start())

    def climbed(step, part):
        climb(step, part).wait_recv()
        if step < 3:
            climb(step + 1, part).start()
            to_right(step, part).start()
            to_left(step, part).start()
        else:
            pl.when(x == 3)(lambda: edge_right(6, part).start())
            pl.when(x > 0)(lambda: edge_left(6, part).start())

    def spread(row, part):
        to_right(row, part).wait_recv()
        pass_keys(row, part).start()
        to_left(row, part).wait_recv()
        pass_values(row, part).start()

    def passed(row):
        for part in range(3):
            pass_keys(row, part).wait_recv()
            pass_values(row, part).wait_recv()

    def got_right(part):
        edge_right(0, part).wait_recv()
        for kind in (0, 1):
            pl.when(far_when[kind])(edge_far(kind, part).start)

    def got_left(part):
        edge_left(0, part).wait_recv()
        for kind in (2, 3):
            pl.when(far_when[kind])(edge_far(kind, part).start)

    def late_edge(part):
        pl.when(x == 0)(lambda: got_right(part))
        pl.when(x < 3)(lambda: got_left(part))

    def give_keys(part, first, count):
        @pl.when(section == 0)
        def _():
            make_keys(first, count)
            hand_keys(part).start()
            own_keys(part).start()
            own_keys(part).wait()

        pl.when(section == 1)(lambda: hand_keys(part).wait_recv())
        begin(part)

    fetch.wait()
    make_queries(0, 1)
    pass_weights(1)
    pass_weights(2)
    for part in range(PIECES):
        for side in range(2):
            row_copy(side, 0, part).wait_recv()
            row_copy(side, 2, part).start()
    pass_weights(3)
    pass_weights(4)
    pl.when(section == 0)(finish_weights)
    give_keys(0, 0, 1)
    for part in range(PIECES):
        for side in range(2):
            row_copy(side, 1, part).wait_recv()
    pl.when(section == 1)(lambda: make_queries(1, 2))
    give_keys(1, 1, 2)
    climbed(0, 0)
    pl.when(section == 0)(lambda: make_queries(1, 2))
    fetch_out.start()
    spread(0, 0)
    climbed(1, 0)
    climbed(0, 1)
    climbed(2, 0)
    spread(1, 0)
    for part in range(PIECES):
        for side in range(2):
            row_copy(side, 2, part).wait_recv()
    give_keys(2, 3, 1)
    spread(0, 1)
    climbed(1, 1)
    make_queries(3, 1)
    swap_queries = start_copy(
        made_queries.at[pl.ds(2 * other, 2)], queries.at[pl.ds(2 * section, 2)],
        swap_s.at[0], swap_r.at[0], section=other,
    )
    own_queries = pltpu.make_async_copy(
        made_queries.at[pl.ds(2 * section, 2)], queries.at[pl.ds(2 * section, 2)], own_s.at[0]
    )
    swap_queries.start()
    own_queries.start()
    climbed(3, 0)
    own_queries.wait()
    swap_queries.wait_recv()

    def token_of(index):
        slot = index // rows
        base = jnp.zeros_like(index)
        for number in range(4):
            base = jnp.where(slot == number, ((place + steps[number]) % 4) * rows, base)
        return base + index % rows

    key_token = token_of(lax.broadcasted_iota(jnp.int32, (1, tokens), 1))
    query_token = shard * tokens + token_of(lax.broadcasted_iota(jnp.int32, (tokens, 1), 0))

    def turn(step):
        if step == 1:
            climbed(0, 2)
            climbed(2, 1)
        elif step == 2:
            spread(2, 0)
            climbed(1, 2)
            for part in range(3):
                pl.when(x > 0)(functools.partial(got_right, part))
                pl.when(x == 3)(functools.partial(got_left, part))
        elif step == 3:
            spread(1, 1)
            spread(0, 2)
        elif step == 5:
            climbed(3, 1)
            climbed(2, 2)
        elif step == 6:
            spread(2, 1)
            climbed(3, 2)
        elif step == 7:
            spread(1, 2)
            late_edge(0)
        elif step == 9:
            passed(0)
        elif step == 10:
            spread(2, 2)
            late_edge(1)
        elif step == 12:
            late_edge(2)
        elif step == 14:
            passed(1)
        elif step == 15:
            passed(2)
        elif step == 16:
            for part in range(3):
                for kind in range(2):
                    edge_far(kind, part).wait_recv()

    def visit(step, carried):
        for number in (1, 2, 3, 5, 6, 7, 9, 10, 12, 14, 15, 16):
            pl.when(step == number)(functools.partial(turn, number))
        keys = meta[0, step] + key_token
        listed = meta[1, step] == 1
        start = jnp.where(listed, starts[:, :1], shard * tokens + tokens)
        seen = (keys >= start) & (keys <= query_token)
        wide[:, :HEAD_WIDTH] = blocks[step, :, HEAD_WIDTH:]
        for head in range(4):
            scores = lax.dot_general(
                queries[head],
                blocks[step, :, :HEAD_WIDTH],
                (((1,), (1,)), ((), ())),
                preferred_element_type=jnp.float32,
            )
            raised = jnp.where(seen, jnp.exp2(jnp.tanh(scores) * RAISE), 0.0)
            total[head] += jnp.dot(
                raised.astype(jnp.bfloat16), wide[...], preferred_element_type=jnp.float32
            )
        return carried

    lax.fori_loop(0, len(SLOTS), visit, 0)

    def swap_back(part):
        span = pl.ds(*BACK[part])
        return start_copy(
            ready.at[span], heads.at[section, span], swap_s.at[1 + part], swap_r.at[1 + part], section=other
        )

    def share_of(owner, low, count, mine):
        value = total[2 * owner + mine, low : low + count, :]
        return (value[:, :HEAD_WIDTH] / value[:, HEAD_WIDTH:]).astype(jnp.bfloat16)

    for part in range(2):
        low, count = BACK[part]
        for mine in range(2):
            lanes = slice(mine * HEAD_WIDTH, (mine + 1) * HEAD_WIDTH)
            ready[low : low + count, lanes] = share_of(other, low, count, mine)
        swap_back(part).start()
    for part in range(2):
        low, count = BACK[part]
        for mine in range(2):
            lanes = slice(mine * HEAD_WIDTH, (mine + 1) * HEAD_WIDTH)
            heads[section, low : low + count, lanes] = share_of(section, low, count, mine)
    fetch_out.wait()
    swap_back(0).wait_recv()

    near_slot = (2, 1)
    inner = 2 * HEAD_WIDTH

    def partial(slot, low):
        span = slice(slot * rows, (slot + 1) * rows)
        return jnp.dot(
            heads[0, span, :], out_weight[:inner, low : low + piece], preferred_element_type=jnp.float32
        ) + jnp.dot(
            heads[1, span, :], out_weight[inner:, low : low + piece], preferred_element_type=jnp.float32
        )

    def send(source, target, sent, landed, side, part):
        return start_copy(
            source.at[side, part], target.at[side, part], sent.at[side, part], landed.at[side, part],
            head=sides[side],
        )

    def far_copy(side, part):
        return send(far_out, far_in, far_s, far_r, side, part)

    def near_copy(side, part):
        return send(near_out, near_in, near_s, near_r, side, part)

    def sum_copy(side, part):
        return send(sum_out, sum_in, sum_s, sum_r, side, part)

    for part in range(PIECES):
        for side in range(2):
            far_out[side, part] = partial(3, side * half + part * piece).astype(jnp.bfloat16)
            far_copy(side, part).start()
    swap_back(1).wait_recv()
    for part in range(PIECES):
        for side in range(2):
            low = (1 - side) * half + part * piece
            near_out[side, part] = partial(near_slot[side], low).astype(jnp.bfloat16)
            near_copy(side, part).start()
    for part in range(PIECES):
        for side in range(2):
            low = side * half + part * piece
            own = partial(near_slot[side], low).astype(jnp.bfloat16).astype(jnp.float32)
            far_copy(side, part).wait_recv()
            sum_out[side, part] = (own + far_in[side, part].astype(jnp.float32)).astype(jnp.bfloat16)
            sum_copy(side, part).start()
    for part in range(2 * PIECES):
        low = part * piece
        mixed[:, low : low + piece] = partial(0, low).astype(jnp.bfloat16).astype(jnp.float32)
    for part in range(PIECES):
        for side in range(2):
            low = (1 - side) * half + part * piece
            near_copy(side, part).wait_recv()
            mixed[:, low : low + piece] += near_in[side, part].astype(jnp.float32)
    squares = jnp.zeros((rows, 128), jnp.float32)
    for part in range(PIECES):
        for side in range(2):
            low = side * half + part * piece
            sum_copy(side, part).wait_recv()
            value = mixed[:, low : low + piece] + sum_in[side, part].astype(jnp.float32)
            mixed[:, low : low + piece] = value
            square = value * value
            for column in range(0, piece, 128):
                squares = squares + square[:, column : column + 128]
    scale = lax.rsqrt(jnp.sum(squares, axis=-1, keepdims=True) / width + epsilon)
    for part in range(2 * PIECES):
        span = slice(part * piece, (part + 1) * piece)
        out_ref[:, span] = (
            hidden_ref[:, span].astype(jnp.float32) + mixed[:, span] * scale * post_ref[:, span]
        ).astype(jnp.bfloat16)

    for side in range(2):
        for part in range(PIECES):
            for kind in range(3):
                row_copy(side, kind, part).wait_send()
            far_copy(side, part).wait_send()
            near_copy(side, part).wait_send()
            sum_copy(side, part).wait_send()
    for part in range(2):
        swap_back(part).wait_send()
    swap_queries.wait_send()
    for part in range(3):
        for step in range(4):
            climb(step, part).wait_send()
        for row in range(3):
            to_right(row, part).wait_send()
            to_left(row, part).wait_send()
            pass_keys(row, part).wait_send()
            pass_values(row, part).wait_send()
        edge_right(0, part).wait_send()
        edge_left(0, part).wait_send()
        for kind in range(4):
            pl.when(far_when[kind])(edge_far(kind, part).wait_send)

    @pl.when(section == 0)
    def _():
        for part in range(3):
            hand_keys(part).wait_send()
        for number in range(3):
            share_across(number).wait_send()
        for at in climbs:
            climb_weights(*at).wait_send()
        for at in second_climbs:
            climb_second(*at).wait_send()
        for back in range(ZS):
            for side in range(2):
                cross_second(side, back).wait_send()
            relay_second(back).wait_send()


def layer(table, hidden, gain, positions, frequency, query_weight, share, out_weight, post_gain):
    rows, width = hidden.shape
    tokens = 4 * rows
    dma = pltpu.SemaphoreType.DMA
    whole = pl.BlockSpec(memory_space=pltpu.VMEM)
    apart = pl.BlockSpec(memory_space=pl.ANY)
    small = pl.BlockSpec(memory_space=pltpu.SMEM)
    pieces = pltpu.VMEM((2, PIECES, rows, width // (2 * PIECES)), jnp.bfloat16)

    def half_type(*shape):
        return pltpu.VMEM(shape, jnp.bfloat16)

    pair = 2 * HEAD_WIDTH
    return pl.pallas_call(
        layer_kernel,
        out_shape=jax.ShapeDtypeStruct((rows, width), jnp.bfloat16),
        in_specs=[small, whole, whole, whole, whole, apart, whole, apart, whole],
        out_specs=whole,
        scratch_shapes=[
            pltpu.SMEM((2, len(SLOTS)), jnp.int32),
            half_type(4, rows, width),
            half_type(*query_weight.shape),
            half_type(width, share.shape[1] * share.shape[2]),
            half_type(*out_weight.shape),
            half_type(4, tokens, HEAD_WIDTH),
            half_type(2, tokens, pair),
            half_type(4, tokens, HEAD_WIDTH),
            half_type(len(SLOTS), tokens, pair),
            pltpu.VMEM((tokens, HEAD_WIDTH), jnp.int32),
            pltpu.VMEM((tokens, HEAD_WIDTH), jnp.float32),
            pltpu.VMEM((tokens, HEAD_WIDTH), jnp.float32),
            pltpu.VMEM((4, tokens, pair), jnp.float32),
            half_type(tokens, pair),
            half_type(tokens, pair),
            half_type(2, tokens, pair),
            pieces, pieces, pieces, pieces, pieces, pieces,
            pltpu.VMEM((rows, width), jnp.float32),
            dma((2,)), dma((2, 3, PIECES)), dma((2, 3, PIECES)), dma((3,)), dma((3,)),
            dma((2, 4, 4)), dma((2, 4, 4)), dma((2, 4)), dma((2, 4)), dma((2, ZS)), dma((2, ZS)), dma((ZS,)), dma((ZS,)),
            dma((3,)), dma((3,)), dma((4,)), dma((3,)), dma((3,)),
            dma((4, 3)), dma((4, 3)), dma((4, 3)), dma((4, 3)), dma((4, 3)), dma((4, 3)),
            dma((3, 3)), dma((3, 3)), dma((3, 3)), dma((3, 3)), dma((4, 3)), dma((2, 3)),
        ]
        + [dma((2, PIECES))] * 6,
        compiler_params=pltpu.CompilerParams(
            collective_id=1, has_side_effects=True, vmem_limit_bytes=62 * 2**20
        ),
        name="layer",
    )(table, hidden, gain, positions, frequency, query_weight, share, out_weight, post_gain)


def local(hidden, q_weight, key_value_weight, o_weight, in_gain, post_gain, positions, block_table):
    lane = jnp.arange(HEAD_WIDTH, dtype=jnp.int32) % (HEAD_WIDTH // 2)
    frequency = 10000.0 ** (-(lane.astype(jnp.float32) * 2.0 / HEAD_WIDTH))
    return layer(
        block_table, hidden[0], in_gain, positions.reshape(-1, hidden.shape[1]), frequency[None],
        q_weight[0], key_value_weight, o_weight[0], post_gain,
    )[None]


def solution(mesh):
    placed = (
        P("section", ("seq", "head"), None),
        P("section", None, "head"),
        P("seq", None, "head"),
        P("section", "head", None),
        P("section", None),
        P("section", None),
        P(),
        P(),
    )
    return jax.shard_map(
        local,
        mesh=mesh,
        in_specs=placed,
        out_specs=P("section", ("seq", "head"), None),
        check_vma=False,
    )
```

```python
import math

import functools

import jax
import jax.numpy as jnp
import numpy as np
from jax import lax
from jax.experimental import pallas as pl
from jax.experimental.pallas import tpu as pltpu
from jax.sharding import PartitionSpec as P

HEAD_WIDTH = 128


epsilon = 1e-06
softcap_limit = 50.0
query_scale = 144.0 ** (-0.5)
RAISE = softcap_limit * math.log2(math.e)
XS, ZS = 4, 8


SLOTS = (
    (0, 0), (1, 0), (2, 0), (1, 1), (1, 3), (3, 0), (4, 0), (2, 1), (2, 3),
    (1, 2), (3, 1), (3, 3), (-1, 1), (-1, 3), (2, 2), (3, 2), (-1, 2),
)
PARTS = ((0, 128), (128, 256), (384, 128))
BACK = ((384, 128), (0, 384))
FIRST = 64
PIECES = 3


def start_copy(source, target, sent, landed, **place):
    copy = pltpu.make_async_remote_copy(
        src_ref=source,
        dst_ref=target,
        send_sem=sent,
        recv_sem=landed,
        device_id=place,
        device_id_type=pl.DeviceIdType.MESH,
    )
    return copy


def greet(places):
    barrier = pltpu.get_barrier_semaphore()
    for place in places:
        pl.semaphore_signal(
            barrier, inc=1, device_id=place, device_id_type=pl.DeviceIdType.MESH
        )
    pl.semaphore_wait(barrier, len(places))


def layer_kernel(
    table, hidden_ref, gain_ref, position_ref, frequency_ref, query_hbm, share_ref, out_hbm, post_ref, out_ref,
    meta, normed, query_weight, kv_weight, out_weight, made_queries, made_kv, queries, blocks, starts, cosine, sine,
    total, wide, ready, heads, far_out, near_out, sum_out, far_in, near_in, sum_in, mixed,
    load, side_s, side_r, x_s, x_r, w_s, w_r, b_s, b_r, c_s, c_r, d_s, d_r, swap_s, swap_r, own_s, hand_s, hand_r,
    z_s, z_r, right_s, right_r, left_s, left_r, key_s, key_r, value_s, value_r, edge_s, edge_r,
    far_s, far_r, near_s, near_r, sum_s, sum_r,
):
    section = lax.axis_index("section")
    shard = lax.axis_index("seq")
    place = lax.axis_index("head")
    other = 1 - section
    z, x = shard // XS, shard % XS
    up = ((z + 1) % ZS) * XS + x
    down = ((z + ZS - 1) % ZS) * XS + x
    across = [z * XS + (x + step) % XS for step in (1, 3, 2)]
    right, left = across[0], across[1]
    rows, width = hidden_ref.shape
    tokens = 4 * rows
    half = width // 2
    piece = half // PIECES
    depth = share_ref.shape[0]
    sides = ((place + 1) % 4, (place + 3) % 4)
    steps = (0, 3, 1, 2)
    fetch = pltpu.make_async_copy(query_hbm, query_weight, load.at[0])
    fetch.start()
    fetch_out = pltpu.make_async_copy(out_hbm, out_weight, load.at[1])
    own_share = pl.ds(pl.multiple_of(shard * depth, 16), depth)
    columns = share_ref.shape[2]
    for number in range(2):
        kv_weight[own_share, number * columns : (number + 1) * columns] = share_ref[:, number, :]
    greet(
        [{"head": sides[0]}, {"head": sides[1]}, {"section": other}]
        + [{"seq": seq} for seq in across + [up, down]]
    )

    def weight_rows(zz, xx, second):
        low = (zz * XS + xx) * depth + (FIRST if second else 0)
        return pl.ds(pl.multiple_of(low, 16), depth - FIRST if second else FIRST)

    def weight_copy(zz, xx, second, sent, landed, seq):
        span = weight_rows(zz % ZS, xx % XS, second)
        return start_copy(kv_weight.at[span], kv_weight.at[span], sent, landed, seq=seq)

    def share_across(number):
        return weight_copy(z, x, False, x_s.at[number], x_r.at[number], across[number])

    def climb_weights(side, hop, aside):
        origin = z + ZS - (hop - 1) if side == 0 else z + (hop - 1)
        return weight_copy(
            origin, x + aside, False, w_s.at[side, hop - 1, aside], w_r.at[side, hop - 1, aside], (up, down)[side]
        )

    climbs = [
        (side, hop, aside)
        for hop in range(1, 5)
        for aside in range(4)
        for side in range(2)
        if hop < 4 or (aside < 2) == (side == 0)
    ]

    def climb_second(side, hop):
        origin = z + ZS - (hop - 1) if side == 0 else z + (hop - 1)
        return weight_copy(origin, x, True, b_s.at[side, hop - 1], b_r.at[side, hop - 1], (up, down)[side])

    second_climbs = [(side, hop) for hop in range(1, 5) for side in range(2) if hop < 4 or side == 0]

    def cross_second(side, back):
        return weight_copy(
            z + ZS - back, x, True, c_s.at[side, back], c_r.at[side, back], (right, left)[side]
        )

    def relay_second(back):
        side = back % 2
        return weight_copy(
            z + ZS - back, x + (3, 1)[side], True, d_s.at[back], d_r.at[back], (right, left)[side]
        )

    def row_copy(side, kind, part):
        which = side if kind == 0 else 1 - side
        span = pl.ds((side if kind == 2 else which) * half + part * piece, piece)
        source = (0, 0, 1 + side)[kind]
        target = (1 + side, 1 + side, 3)[kind]
        return start_copy(
            normed.at[source, :, span], normed.at[target, :, span],
            side_s.at[side, kind, part], side_r.at[side, kind, part], head=sides[side],
        )

    @pl.when(section == 0)
    def _():
        for number in range(3):
            share_across(number).start()
        for side in range(2):
            climb_second(side, 1).start()
            climb_weights(side, 1, 0).start()
            cross_second(side, 0).start()

    squares = jnp.zeros((rows, 128), jnp.float32)
    for column in range(0, width, 128):
        value = hidden_ref[:, column : column + 128].astype(jnp.float32)
        squares = squares + value * value
    scale = lax.rsqrt(jnp.sum(squares, axis=-1, keepdims=True) / width + epsilon)
    for part in range(2 * PIECES):
        span = slice(part * piece, (part + 1) * piece)
        normed[0, :, span] = (
            hidden_ref[:, span].astype(jnp.float32) * scale * gain_ref[:, span]
        ).astype(jnp.bfloat16)
    for kind in range(2):
        for part in range(PIECES):
            for side in range(2):
                row_copy(side, kind, part).start()

    @pl.when(section == 0)
    def _():
        for number, aside in ((0, 3), (1, 1), (2, 2)):
            share_across(number).wait_recv()
            for side in range(2):
                climb_weights(side, 1, aside).start()

    for number, (back, aside) in enumerate(SLOTS):
        source = (x + XS - aside) % XS
        row = jnp.where(source < x, 0, 4) if back < 0 else back
        block = (z - row) * XS + source
        meta[0, number] = block * tokens
        meta[1, number] = table[shard, jnp.maximum(block, 0)]
    def product(first, count, weight, low):
        return jnp.dot(
            normed[first : first + count].reshape(count * rows, width),
            weight[:, low : low + 2 * HEAD_WIDTH],
            preferred_element_type=jnp.float32,
        )

    def turned(value, span):
        return value * cosine[span, :] + pltpu.roll(value, HEAD_WIDTH // 2, 1) * sine[span, :]

    def make_queries(first, count):
        for pair in range(2):
            result = product(first, count, query_weight, pair * 2 * HEAD_WIDTH)
            for slot in range(count):
                low = (first + slot) * rows
                for mine in range(2):
                    value = result[slot * rows : (slot + 1) * rows, mine * HEAD_WIDTH : (mine + 1) * HEAD_WIDTH]
                    made_queries[2 * pair + mine, low : low + rows, :] = (
                        turned(value, slice(low, low + rows)) * (query_scale / softcap_limit)
                    ).astype(jnp.bfloat16)

    def make_keys(first, count):
        for pair in range(2):
            result = product(first, count, kv_weight, pair * 2 * HEAD_WIDTH)
            for slot in range(count):
                low = (first + slot) * rows
                for mine in range(2):
                    value = result[slot * rows : (slot + 1) * rows, mine * HEAD_WIDTH : (mine + 1) * HEAD_WIDTH]
                    if pair == 0:
                        value = turned(value, slice(low, low + rows))
                    made_kv[mine, low : low + rows, pair * HEAD_WIDTH : (pair + 1) * HEAD_WIDTH] = value.astype(
                        jnp.bfloat16
                    )

    def pass_weights(hop):
        @pl.when(section == 0)
        def _():
            for side, at in second_climbs:
                if at == hop:
                    climb_second(side, hop).wait_recv()
                    if (side, hop + 1) in second_climbs:
                        climb_second(side, hop + 1).start()
                    for across_side in range(2):
                        cross_second(across_side, hop if side == 0 else ZS - hop).start()
            for side, at, aside in climbs:
                if at == hop:
                    climb_weights(side, hop, aside).wait_recv()
                    if (side, hop + 1, aside) in climbs:
                        climb_weights(side, hop + 1, aside).start()
            for back in ((0,), (1, 7), (2, 6), (3, 5), (4,))[hop - 1]:
                for side in range(2):
                    cross_second(side, back).wait_recv()
                relay_second(back).start()

    def finish_weights():
        for side in range(2):
            cross_second(side, 4).wait_recv()
        relay_second(4).start()
        for back in range(ZS):
            relay_second(back).wait_recv()

    def span_of(part):
        return pl.ds(*PARTS[part])

    def hand_keys(part):
        span = span_of(part)
        return start_copy(
            made_kv.at[1, span], blocks.at[0, span], hand_s.at[part], hand_r.at[part], section=other
        )

    def own_keys(part):
        span = span_of(part)
        return pltpu.make_async_copy(made_kv.at[0, span], blocks.at[0, span], own_s.at[1 + part])

    def block_copy(source, target, part, sent, landed, seq, columns=(0, 2 * HEAD_WIDTH)):
        span, width_of = span_of(part), pl.ds(*columns)
        return start_copy(
            blocks.at[source, span, width_of], blocks.at[target, span, width_of], sent, landed, seq=seq
        )

    def climb(step, part):
        slots = (0, 1, 2, 5, 6)
        return block_copy(slots[step], slots[step + 1], part, z_s.at[step, part], z_r.at[step, part], up)

    def to_right(row, part):
        source, target = ((1, 3), (2, 7), (5, 10))[row]
        return block_copy(source, target, part, right_s.at[row, part], right_r.at[row, part], right)

    def to_left(row, part):
        source, target = ((1, 4), (2, 8), (5, 11))[row]
        return block_copy(source, target, part, left_s.at[row, part], left_r.at[row, part], left)

    keys_of, values_of = (0, HEAD_WIDTH), (HEAD_WIDTH, HEAD_WIDTH)

    def pass_keys(row, part):
        source, target = ((3, 9), (7, 14), (10, 15))[row]
        return block_copy(source, target, part, key_s.at[row, part], key_r.at[row, part], right, keys_of)

    def pass_values(row, part):
        source, target = ((4, 9), (8, 14), (11, 15))[row]
        return block_copy(source, target, part, value_s.at[row, part], value_r.at[row, part], left, values_of)

    def edge_right(source, part):
        return block_copy(source, 12, part, right_s.at[3, part], right_r.at[3, part], right)

    def edge_left(source, part):
        return block_copy(source, 13, part, left_s.at[3, part], left_r.at[3, part], left)

    def edge_far(kind, part):
        return block_copy(
            (12, 12, 13, 13)[kind], 16, part, edge_s.at[kind, part], edge_r.at[kind % 2, part],
            (right, right, left, left)[kind], (keys_of, values_of)[kind % 2],
        )

    far_when = (x < 3, x == 2, x == 1, x > 0)

    def begin(part):
        climb(0, part).start()
        pl.when(x < 3)(lambda: edge_right(0, part).start())
        pl.when(x == 0)(lambda: edge_left(0, part).start())

    def climbed(step, part):
        climb(step, part).wait_recv()
        if step < 3:
            climb(step + 1, part).start()
            to_right(step, part).start()
            to_left(step, part).start()
        else:
            pl.when(x == 3)(lambda: edge_right(6, part).start())
            pl.when(x > 0)(lambda: edge_left(6, part).start())

    def spread(row, part):
        to_right(row, part).wait_recv()
        pass_keys(row, part).start()
        to_left(row, part).wait_recv()
        pass_values(row, part).start()

    def passed(row):
        for part in range(3):
            pass_keys(row, part).wait_recv()
            pass_values(row, part).wait_recv()

    def got_right(part):
        edge_right(0, part).wait_recv()
        for kind in (0, 1):
            pl.when(far_when[kind])(edge_far(kind, part).start)

    def got_left(part):
        edge_left(0, part).wait_recv()
        for kind in (2, 3):
            pl.when(far_when[kind])(edge_far(kind, part).start)

    def late_edge(part):
        pl.when(x == 0)(lambda: got_right(part))
        pl.when(x < 3)(lambda: got_left(part))

    def give_keys(part, first, count):
        @pl.when(section == 0)
        def _():
            make_keys(first, count)
            hand_keys(part).start()
            own_keys(part).start()
            own_keys(part).wait()

        pl.when(section == 1)(lambda: hand_keys(part).wait_recv())
        begin(part)

    pass_weights(1)
    pass_weights(2)
    lane = lax.broadcasted_iota(jnp.int32, (rows, HEAD_WIDTH), 1)
    line = lax.broadcasted_iota(jnp.int32, (rows, HEAD_WIDTH), 0)
    for slot in range(4):
        origin = (place + steps[slot]) % 4
        span = slice(slot * rows, (slot + 1) * rows)
        at = jnp.transpose(jnp.broadcast_to(position_ref[pl.ds(4 * shard + origin, 1), :], (rows, rows)))
        starts[span, :] = shard * tokens + origin * rows + line - at
        angle = at.astype(jnp.float32) * frequency_ref[...]
        cosine[span, :] = jnp.cos(angle)
        sine[span, :] = jnp.sin(angle) * jnp.where(lane < HEAD_WIDTH // 2, -1.0, 1.0)
    pass_weights(3)
    for part in range(PIECES):
        for side in range(2):
            row_copy(side, 0, part).wait_recv()
            row_copy(side, 2, part).start()
    pass_weights(4)
    pl.when(section == 0)(finish_weights)
    give_keys(0, 0, 1)
    fetch.wait()
    make_queries(0, 1)
    total[...] = jnp.zeros_like(total)
    wide[...] = jnp.ones_like(wide)

    for part in range(PIECES):
        for side in range(2):
            row_copy(side, 1, part).wait_recv()
    climbed(0, 0)
    pl.when(section == 1)(lambda: make_queries(1, 2))
    give_keys(1, 1, 2)
    spread(0, 0)
    climbed(1, 0)
    fetch_out.start()
    pl.when(section == 0)(lambda: make_queries(1, 2))
    climbed(2, 0)
    climbed(0, 1)
    spread(1, 0)
    for part in range(PIECES):
        for side in range(2):
            row_copy(side, 2, part).wait_recv()
    give_keys(2, 3, 1)
    spread(0, 1)
    climbed(1, 1)
    make_queries(3, 1)
    swap_queries = start_copy(
        made_queries.at[pl.ds(2 * other, 2)], queries.at[pl.ds(2 * section, 2)],
        swap_s.at[0], swap_r.at[0], section=other,
    )
    own_queries = pltpu.make_async_copy(
        made_queries.at[pl.ds(2 * section, 2)], queries.at[pl.ds(2 * section, 2)], own_s.at[0]
    )
    swap_queries.start()
    own_queries.start()
    climbed(3, 0)
    own_queries.wait()
    swap_queries.wait_recv()

    def token_of(index):
        slot = index // rows
        base = jnp.zeros_like(index)
        for number in range(4):
            base = jnp.where(slot == number, ((place + steps[number]) % 4) * rows, base)
        return base + index % rows

    key_token = token_of(lax.broadcasted_iota(jnp.int32, (1, tokens), 1))
    query_token = shard * tokens + token_of(lax.broadcasted_iota(jnp.int32, (tokens, 1), 0))

    def turn(step):
        if step == 1:
            climbed(0, 2)
            climbed(2, 1)
        elif step == 2:
            spread(2, 0)
            climbed(1, 2)
            for part in range(3):
                pl.when(x > 0)(functools.partial(got_right, part))
                pl.when(x == 3)(functools.partial(got_left, part))
        elif step == 3:
            spread(1, 1)
            spread(0, 2)
        elif step == 5:
            climbed(3, 1)
            climbed(2, 2)
        elif step == 6:
            spread(2, 1)
            climbed(3, 2)
        elif step == 7:
            spread(1, 2)
            late_edge(0)
        elif step == 9:
            passed(0)
        elif step == 10:
            spread(2, 2)
            late_edge(1)
        elif step == 12:
            late_edge(2)
        elif step == 14:
            passed(1)
        elif step == 15:
            passed(2)
        elif step == 16:
            for part in range(3):
                for kind in range(2):
                    edge_far(kind, part).wait_recv()

    def visit(step, carried):
        for number in (1, 2, 3, 5, 6, 7, 9, 10, 12, 14, 15, 16):
            pl.when(step == number)(functools.partial(turn, number))
        keys = meta[0, step] + key_token
        listed = meta[1, step] == 1
        start = jnp.where(listed, starts[:, :1], shard * tokens + tokens)
        seen = (keys >= start) & (keys <= query_token)
        wide[:, :HEAD_WIDTH] = blocks[step, :, HEAD_WIDTH:]
        for head in range(4):
            scores = lax.dot_general(
                queries[head],
                blocks[step, :, :HEAD_WIDTH],
                (((1,), (1,)), ((), ())),
                preferred_element_type=jnp.float32,
            )
            raised = jnp.where(seen, jnp.exp2(jnp.tanh(scores) * RAISE), 0.0)
            total[head] += jnp.dot(
                raised.astype(jnp.bfloat16), wide[...], preferred_element_type=jnp.float32
            )
        return carried

    lax.fori_loop(0, len(SLOTS), visit, 0)

    def swap_back(part):
        span = pl.ds(*BACK[part])
        return start_copy(
            ready.at[span], heads.at[section, span], swap_s.at[1 + part], swap_r.at[1 + part], section=other
        )

    def share_of(owner, low, count, mine):
        value = total[2 * owner + mine, low : low + count, :]
        return (value[:, :HEAD_WIDTH] / value[:, HEAD_WIDTH:]).astype(jnp.bfloat16)

    for part in range(2):
        low, count = BACK[part]
        for mine in range(2):
            lanes = slice(mine * HEAD_WIDTH, (mine + 1) * HEAD_WIDTH)
            ready[low : low + count, lanes] = share_of(other, low, count, mine)
        swap_back(part).start()
    for part in range(2):
        low, count = BACK[part]
        for mine in range(2):
            lanes = slice(mine * HEAD_WIDTH, (mine + 1) * HEAD_WIDTH)
            heads[section, low : low + count, lanes] = share_of(section, low, count, mine)
    fetch_out.wait()
    swap_back(0).wait_recv()

    near_slot = (2, 1)
    inner = 2 * HEAD_WIDTH

    def partial(slot, low):
        span = slice(slot * rows, (slot + 1) * rows)
        return jnp.dot(
            heads[0, span, :], out_weight[:inner, low : low + piece], preferred_element_type=jnp.float32
        ) + jnp.dot(
            heads[1, span, :], out_weight[inner:, low : low + piece], preferred_element_type=jnp.float32
        )

    def send(source, target, sent, landed, side, part):
        return start_copy(
            source.at[side, part], target.at[side, part], sent.at[side, part], landed.at[side, part],
            head=sides[side],
        )

    def far_copy(side, part):
        return send(far_out, far_in, far_s, far_r, side, part)

    def near_copy(side, part):
        return send(near_out, near_in, near_s, near_r, side, part)

    def sum_copy(side, part):
        return send(sum_out, sum_in, sum_s, sum_r, side, part)

    for part in range(PIECES):
        for side in range(2):
            far_out[side, part] = partial(3, side * half + part * piece).astype(jnp.bfloat16)
            far_copy(side, part).start()
    swap_back(1).wait_recv()
    for part in range(PIECES):
        for side in range(2):
            low = (1 - side) * half + part * piece
            near_out[side, part] = partial(near_slot[side], low).astype(jnp.bfloat16)
            near_copy(side, part).start()
    for part in range(PIECES):
        for side in range(2):
            low = side * half + part * piece
            own = partial(near_slot[side], low).astype(jnp.bfloat16).astype(jnp.float32)
            far_copy(side, part).wait_recv()
            sum_out[side, part] = (own + far_in[side, part].astype(jnp.float32)).astype(jnp.bfloat16)
            sum_copy(side, part).start()
    for part in range(2 * PIECES):
        low = part * piece
        mixed[:, low : low + piece] = partial(0, low).astype(jnp.bfloat16).astype(jnp.float32)
    for part in range(PIECES):
        for side in range(2):
            low = (1 - side) * half + part * piece
            near_copy(side, part).wait_recv()
            mixed[:, low : low + piece] += near_in[side, part].astype(jnp.float32)
    squares = jnp.zeros((rows, 128), jnp.float32)
    for part in range(PIECES):
        for side in range(2):
            low = side * half + part * piece
            sum_copy(side, part).wait_recv()
            value = mixed[:, low : low + piece] + sum_in[side, part].astype(jnp.float32)
            mixed[:, low : low + piece] = value
            square = value * value
            for column in range(0, piece, 128):
                squares = squares + square[:, column : column + 128]
    scale = lax.rsqrt(jnp.sum(squares, axis=-1, keepdims=True) / width + epsilon)
    for part in range(2 * PIECES):
        span = slice(part * piece, (part + 1) * piece)
        out_ref[:, span] = (
            hidden_ref[:, span].astype(jnp.float32) + mixed[:, span] * scale * post_ref[:, span]
        ).astype(jnp.bfloat16)

    for side in range(2):
        for part in range(PIECES):
            for kind in range(3):
                row_copy(side, kind, part).wait_send()
            far_copy(side, part).wait_send()
            near_copy(side, part).wait_send()
            sum_copy(side, part).wait_send()
    for part in range(2):
        swap_back(part).wait_send()
    swap_queries.wait_send()
    for part in range(3):
        for step in range(4):
            climb(step, part).wait_send()
        for row in range(3):
            to_right(row, part).wait_send()
            to_left(row, part).wait_send()
            pass_keys(row, part).wait_send()
            pass_values(row, part).wait_send()
        edge_right(0, part).wait_send()
        edge_left(0, part).wait_send()
        for kind in range(4):
            pl.when(far_when[kind])(edge_far(kind, part).wait_send)

    @pl.when(section == 0)
    def _():
        for part in range(3):
            hand_keys(part).wait_send()
        for number in range(3):
            share_across(number).wait_send()
        for at in climbs:
            climb_weights(*at).wait_send()
        for at in second_climbs:
            climb_second(*at).wait_send()
        for back in range(ZS):
            for side in range(2):
                cross_second(side, back).wait_send()
            relay_second(back).wait_send()


def layer(table, hidden, gain, positions, frequency, query_weight, share, out_weight, post_gain):
    rows, width = hidden.shape
    tokens = 4 * rows
    dma = pltpu.SemaphoreType.DMA
    whole = pl.BlockSpec(memory_space=pltpu.VMEM)
    apart = pl.BlockSpec(memory_space=pl.ANY)
    small = pl.BlockSpec(memory_space=pltpu.SMEM)
    pieces = pltpu.VMEM((2, PIECES, rows, width // (2 * PIECES)), jnp.bfloat16)

    def half_type(*shape):
        return pltpu.VMEM(shape, jnp.bfloat16)

    pair = 2 * HEAD_WIDTH
    return pl.pallas_call(
        layer_kernel,
        out_shape=jax.ShapeDtypeStruct((rows, width), jnp.bfloat16),
        in_specs=[small, whole, whole, whole, whole, apart, whole, apart, whole],
        out_specs=whole,
        scratch_shapes=[
            pltpu.SMEM((2, len(SLOTS)), jnp.int32),
            half_type(4, rows, width),
            half_type(*query_weight.shape),
            half_type(width, share.shape[1] * share.shape[2]),
            half_type(*out_weight.shape),
            half_type(4, tokens, HEAD_WIDTH),
            half_type(2, tokens, pair),
            half_type(4, tokens, HEAD_WIDTH),
            half_type(len(SLOTS), tokens, pair),
            pltpu.VMEM((tokens, HEAD_WIDTH), jnp.int32),
            pltpu.VMEM((tokens, HEAD_WIDTH), jnp.float32),
            pltpu.VMEM((tokens, HEAD_WIDTH), jnp.float32),
            pltpu.VMEM((4, tokens, pair), jnp.float32),
            half_type(tokens, pair),
            half_type(tokens, pair),
            half_type(2, tokens, pair),
            pieces, pieces, pieces, pieces, pieces, pieces,
            pltpu.VMEM((rows, width), jnp.float32),
            dma((2,)), dma((2, 3, PIECES)), dma((2, 3, PIECES)), dma((3,)), dma((3,)),
            dma((2, 4, 4)), dma((2, 4, 4)), dma((2, 4)), dma((2, 4)), dma((2, ZS)), dma((2, ZS)), dma((ZS,)), dma((ZS,)),
            dma((3,)), dma((3,)), dma((4,)), dma((3,)), dma((3,)),
            dma((4, 3)), dma((4, 3)), dma((4, 3)), dma((4, 3)), dma((4, 3)), dma((4, 3)),
            dma((3, 3)), dma((3, 3)), dma((3, 3)), dma((3, 3)), dma((4, 3)), dma((2, 3)),
        ]
        + [dma((2, PIECES))] * 6,
        compiler_params=pltpu.CompilerParams(
            collective_id=1, has_side_effects=True, vmem_limit_bytes=62 * 2**20
        ),
        name="layer",
    )(table, hidden, gain, positions, frequency, query_weight, share, out_weight, post_gain)


def local(hidden, q_weight, key_value_weight, o_weight, in_gain, post_gain, positions, block_table):
    lane = np.arange(HEAD_WIDTH) % (HEAD_WIDTH // 2)
    frequency = jnp.asarray((10000.0 ** (-lane * 2.0 / HEAD_WIDTH)).astype(np.float32))
    return layer(
        block_table, hidden[0], in_gain, positions.reshape(-1, hidden.shape[1]), frequency[None],
        q_weight[0], key_value_weight, o_weight[0], post_gain,
    )[None]


def solution(mesh):
    placed = (
        P("section", ("seq", "head"), None),
        P("section", None, "head"),
        P("seq", None, "head"),
        P("section", "head", None),
        P("section", None),
        P("section", None),
        P(),
        P(),
    )
    return jax.shard_map(
        local,
        mesh=mesh,
        in_specs=placed,
        out_specs=P("section", ("seq", "head"), None),
        check_vma=False,
    )
```

```python
import math

import functools

import jax
import jax.numpy as jnp
import numpy as np
from jax import lax
from jax.experimental import pallas as pl
from jax.experimental.pallas import tpu as pltpu
from jax.sharding import PartitionSpec as P

HEAD_WIDTH = 128


epsilon = 1e-06
softcap_limit = 50.0
query_scale = 144.0 ** (-0.5)
RAISE = softcap_limit * math.log2(math.e)
XS, ZS = 4, 8


SLOTS = (
    (0, 0), (1, 0), (2, 0), (1, 1), (1, 3), (3, 0), (4, 0), (2, 1), (2, 3),
    (1, 2), (3, 1), (3, 3), (-1, 1), (-1, 3), (2, 2), (3, 2), (-1, 2),
)
PARTS = ((0, 128), (128, 256), (384, 128))
BACK = ((384, 128), (0, 384))
FIRST = 64
PIECES = 3


def start_copy(source, target, sent, landed, **place):
    copy = pltpu.make_async_remote_copy(
        src_ref=source,
        dst_ref=target,
        send_sem=sent,
        recv_sem=landed,
        device_id=place,
        device_id_type=pl.DeviceIdType.MESH,
    )
    return copy


def greet(places):
    barrier = pltpu.get_barrier_semaphore()
    for place in places:
        pl.semaphore_signal(
            barrier, inc=1, device_id=place, device_id_type=pl.DeviceIdType.MESH
        )
    pl.semaphore_wait(barrier, len(places))


def layer_kernel(
    table, hidden_ref, gain_ref, position_ref, frequency_ref, query_hbm, share_ref, out_hbm, post_ref, out_ref,
    meta, normed, query_weight, kv_weight, out_weight, made_queries, made_kv, queries, blocks, starts, cosine, sine,
    total, wide, ready, heads, far_out, near_out, sum_out, far_in, near_in, sum_in, mixed,
    load, side_s, side_r, x_s, x_r, w_s, w_r, b_s, b_r, c_s, c_r, d_s, d_r, swap_s, swap_r, own_s, hand_s, hand_r,
    z_s, z_r, right_s, right_r, left_s, left_r, key_s, key_r, value_s, value_r, edge_s, edge_r,
    far_s, far_r, near_s, near_r, sum_s, sum_r,
):
    section = lax.axis_index("section")
    shard = lax.axis_index("seq")
    place = lax.axis_index("head")
    other = 1 - section
    z, x = shard // XS, shard % XS
    up = ((z + 1) % ZS) * XS + x
    down = ((z + ZS - 1) % ZS) * XS + x
    across = [z * XS + (x + step) % XS for step in (1, 3, 2)]
    right, left = across[0], across[1]
    rows, width = hidden_ref.shape
    tokens = 4 * rows
    half = width // 2
    piece = half // PIECES
    depth = share_ref.shape[0]
    sides = ((place + 1) % 4, (place + 3) % 4)
    steps = (0, 3, 1, 2)
    fetch = pltpu.make_async_copy(query_hbm, query_weight, load.at[0])
    fetch.start()
    fetch_out = pltpu.make_async_copy(out_hbm, out_weight, load.at[1])
    own_share = pl.ds(pl.multiple_of(shard * depth, 16), depth)
    columns = share_ref.shape[2]
    for number in range(2):
        kv_weight[own_share, number * columns : (number + 1) * columns] = share_ref[:, number, :]
    greet(
        [{"head": sides[0]}, {"head": sides[1]}, {"section": other}]
        + [{"seq": seq} for seq in across + [up, down]]
    )

    def weight_rows(zz, xx, second):
        low = (zz * XS + xx) * depth + (FIRST if second else 0)
        return pl.ds(pl.multiple_of(low, 16), depth - FIRST if second else FIRST)

    def weight_copy(zz, xx, second, sent, landed, seq):
        span = weight_rows(zz % ZS, xx % XS, second)
        return start_copy(kv_weight.at[span], kv_weight.at[span], sent, landed, seq=seq)

    def share_across(number):
        return weight_copy(z, x, False, x_s.at[number], x_r.at[number], across[number])

    def climb_weights(side, hop, aside):
        origin = z + ZS - (hop - 1) if side == 0 else z + (hop - 1)
        return weight_copy(
            origin, x + aside, False, w_s.at[side, hop - 1, aside], w_r.at[side, hop - 1, aside], (up, down)[side]
        )

    climbs = [
        (side, hop, aside)
        for hop in range(1, 5)
        for aside in range(4)
        for side in range(2)
        if hop < 4 or (aside < 2) == (side == 0)
    ]

    def climb_second(side, hop):
        origin = z + ZS - (hop - 1) if side == 0 else z + (hop - 1)
        return weight_copy(origin, x, True, b_s.at[side, hop - 1], b_r.at[side, hop - 1], (up, down)[side])

    second_climbs = [(side, hop) for hop in range(1, 5) for side in range(2) if hop < 4 or side == 0]

    def cross_second(side, back):
        return weight_copy(
            z + ZS - back, x, True, c_s.at[side, back], c_r.at[side, back], (right, left)[side]
        )

    def relay_second(back):
        side = back % 2
        return weight_copy(
            z + ZS - back, x + (3, 1)[side], True, d_s.at[back], d_r.at[back], (right, left)[side]
        )

    def row_copy(side, kind, part):
        which = side if kind == 0 else 1 - side
        span = pl.ds((side if kind == 2 else which) * half + part * piece, piece)
        source = (0, 0, 1 + side)[kind]
        target = (1 + side, 1 + side, 3)[kind]
        return start_copy(
            normed.at[source, :, span], normed.at[target, :, span],
            side_s.at[side, kind, part], side_r.at[side, kind, part], head=sides[side],
        )

    @pl.when(section == 0)
    def _():
        for number in range(3):
            share_across(number).start()
        for side in range(2):
            climb_second(side, 1).start()
            climb_weights(side, 1, 0).start()
            cross_second(side, 0).start()

    squares = jnp.zeros((rows, 128), jnp.float32)
    for column in range(0, width, 128):
        value = hidden_ref[:, column : column + 128].astype(jnp.float32)
        squares = squares + value * value
    scale = lax.rsqrt(jnp.sum(squares, axis=-1, keepdims=True) / width + epsilon)
    for part in range(2 * PIECES):
        span = slice(part * piece, (part + 1) * piece)
        normed[0, :, span] = (
            hidden_ref[:, span].astype(jnp.float32) * scale * gain_ref[:, span]
        ).astype(jnp.bfloat16)
    for kind in range(2):
        for part in range(PIECES):
            for side in range(2):
                row_copy(side, kind, part).start()

    @pl.when(section == 0)
    def _():
        for number, aside in ((0, 3), (1, 1), (2, 2)):
            share_across(number).wait_recv()
            for side in range(2):
                climb_weights(side, 1, aside).start()

    for number, (back, aside) in enumerate(SLOTS):
        source = (x + XS - aside) % XS
        row = jnp.where(source < x, 0, 4) if back < 0 else back
        block = (z - row) * XS + source
        meta[0, number] = block * tokens
        meta[1, number] = table[shard, jnp.maximum(block, 0)]
    def product(first, count, weight, low):
        return jnp.dot(
            normed[first : first + count].reshape(count * rows, width),
            weight[:, low : low + 2 * HEAD_WIDTH],
            preferred_element_type=jnp.float32,
        )

    def turned(value, span):
        return value * cosine[span, :] + pltpu.roll(value, HEAD_WIDTH // 2, 1) * sine[span, :]

    def make_queries(first, count):
        for pair in range(2):
            result = product(first, count, query_weight, pair * 2 * HEAD_WIDTH)
            for slot in range(count):
                low = (first + slot) * rows
                for mine in range(2):
                    value = result[slot * rows : (slot + 1) * rows, mine * HEAD_WIDTH : (mine + 1) * HEAD_WIDTH]
                    made_queries[2 * pair + mine, low : low + rows, :] = (
                        turned(value, slice(low, low + rows)) * (query_scale / softcap_limit)
                    ).astype(jnp.bfloat16)

    def make_keys(first, count):
        for pair in range(2):
            result = product(first, count, kv_weight, pair * 2 * HEAD_WIDTH)
            for slot in range(count):
                low = (first + slot) * rows
                for mine in range(2):
                    value = result[slot * rows : (slot + 1) * rows, mine * HEAD_WIDTH : (mine + 1) * HEAD_WIDTH]
                    if pair == 0:
                        value = turned(value, slice(low, low + rows))
                    made_kv[mine, low : low + rows, pair * HEAD_WIDTH : (pair + 1) * HEAD_WIDTH] = value.astype(
                        jnp.bfloat16
                    )

    def pass_weights(hop):
        @pl.when(section == 0)
        def _():
            for side, at in second_climbs:
                if at == hop:
                    climb_second(side, hop).wait_recv()
                    if (side, hop + 1) in second_climbs:
                        climb_second(side, hop + 1).start()
                    for across_side in range(2):
                        cross_second(across_side, hop if side == 0 else ZS - hop).start()
            for side, at, aside in climbs:
                if at == hop:
                    climb_weights(side, hop, aside).wait_recv()
                    if (side, hop + 1, aside) in climbs:
                        climb_weights(side, hop + 1, aside).start()
            for back in ((0,), (1, 7), (2, 6), (3, 5), (4,))[hop - 1]:
                for side in range(2):
                    cross_second(side, back).wait_recv()
                relay_second(back).start()

    def finish_weights():
        for side in range(2):
            cross_second(side, 4).wait_recv()
        relay_second(4).start()
        for back in range(ZS):
            relay_second(back).wait_recv()

    def span_of(part):
        return pl.ds(*PARTS[part])

    def hand_keys(part):
        span = span_of(part)
        return start_copy(
            made_kv.at[1, span], blocks.at[0, span], hand_s.at[part], hand_r.at[part], section=other
        )

    def own_keys(part):
        span = span_of(part)
        return pltpu.make_async_copy(made_kv.at[0, span], blocks.at[0, span], own_s.at[1 + part])

    def block_copy(source, target, part, sent, landed, seq, columns=(0, 2 * HEAD_WIDTH)):
        span, width_of = span_of(part), pl.ds(*columns)
        return start_copy(
            blocks.at[source, span, width_of], blocks.at[target, span, width_of], sent, landed, seq=seq
        )

    def climb(step, part):
        slots = (0, 1, 2, 5, 6)
        return block_copy(slots[step], slots[step + 1], part, z_s.at[step, part], z_r.at[step, part], up)

    def to_right(row, part):
        source, target = ((1, 3), (2, 7), (5, 10))[row]
        return block_copy(source, target, part, right_s.at[row, part], right_r.at[row, part], right)

    def to_left(row, part):
        source, target = ((1, 4), (2, 8), (5, 11))[row]
        return block_copy(source, target, part, left_s.at[row, part], left_r.at[row, part], left)

    keys_of, values_of = (0, HEAD_WIDTH), (HEAD_WIDTH, HEAD_WIDTH)

    def pass_keys(row, part):
        source, target = ((3, 9), (7, 14), (10, 15))[row]
        return block_copy(source, target, part, key_s.at[row, part], key_r.at[row, part], right, keys_of)

    def pass_values(row, part):
        source, target = ((4, 9), (8, 14), (11, 15))[row]
        return block_copy(source, target, part, value_s.at[row, part], value_r.at[row, part], left, values_of)

    def edge_right(source, part):
        return block_copy(source, 12, part, right_s.at[3, part], right_r.at[3, part], right)

    def edge_left(source, part):
        return block_copy(source, 13, part, left_s.at[3, part], left_r.at[3, part], left)

    def far_up(part):
        return block_copy(15, 16, part, edge_s.at[part], edge_r.at[part], up)

    def far_down(part):
        return block_copy(9, 16, part, edge_s.at[part], edge_r.at[part], down)

    def begin(part):
        climb(0, part).start()
        pl.when(x < 3)(lambda: edge_right(0, part).start())
        pl.when(x == 0)(lambda: edge_left(0, part).start())

    def climbed(step, part):
        climb(step, part).wait_recv()
        if step < 3:
            climb(step + 1, part).start()
            to_right(step, part).start()
            to_left(step, part).start()
        else:
            pl.when(x == 3)(lambda: edge_right(6, part).start())
            pl.when(x > 0)(lambda: edge_left(6, part).start())

    def spread(row, part):
        to_right(row, part).wait_recv()
        pass_keys(row, part).start()
        to_left(row, part).wait_recv()
        pass_values(row, part).start()

    def passed(row, part):
        pass_keys(row, part).wait_recv()
        pass_values(row, part).wait_recv()
        if row == 0:
            pl.when(x > 1)(far_down(part).start)
        elif row == 2:
            pl.when(x < 2)(far_up(part).start)

    def got_right(part):
        edge_right(0, part).wait_recv()

    def got_left(part):
        edge_left(0, part).wait_recv()

    def late_edge(part):
        pl.when(x == 0)(lambda: got_right(part))
        pl.when(x < 3)(lambda: got_left(part))

    def give_keys(part, first, count):
        @pl.when(section == 0)
        def _():
            make_keys(first, count)
            hand_keys(part).start()
            own_keys(part).start()
            own_keys(part).wait()

        pl.when(section == 1)(lambda: hand_keys(part).wait_recv())
        begin(part)

    pass_weights(1)
    pass_weights(2)
    lane = lax.broadcasted_iota(jnp.int32, (rows, HEAD_WIDTH), 1)
    line = lax.broadcasted_iota(jnp.int32, (rows, HEAD_WIDTH), 0)
    for slot in range(4):
        origin = (place + steps[slot]) % 4
        span = slice(slot * rows, (slot + 1) * rows)
        at = jnp.transpose(jnp.broadcast_to(position_ref[pl.ds(4 * shard + origin, 1), :], (rows, rows)))
        starts[span, :] = shard * tokens + origin * rows + line - at
        angle = at.astype(jnp.float32) * frequency_ref[...]
        cosine[span, :] = jnp.cos(angle)
        sine[span, :] = jnp.sin(angle) * jnp.where(lane < HEAD_WIDTH // 2, -1.0, 1.0)
    pass_weights(3)
    for part in range(PIECES):
        for side in range(2):
            row_copy(side, 0, part).wait_recv()
            row_copy(side, 2, part).start()
    pass_weights(4)
    pl.when(section == 0)(finish_weights)
    give_keys(0, 0, 1)
    fetch.wait()
    make_queries(0, 1)
    total[...] = jnp.zeros_like(total)
    wide[...] = jnp.ones_like(wide)

    for part in range(PIECES):
        for side in range(2):
            row_copy(side, 1, part).wait_recv()
    climbed(0, 0)
    pl.when(section == 1)(lambda: make_queries(1, 2))
    give_keys(1, 1, 2)
    spread(0, 0)
    climbed(1, 0)
    fetch_out.start()
    pl.when(section == 0)(lambda: make_queries(1, 2))
    climbed(2, 0)
    climbed(0, 1)
    spread(1, 0)
    for part in range(PIECES):
        for side in range(2):
            row_copy(side, 2, part).wait_recv()
    give_keys(2, 3, 1)
    spread(0, 1)
    climbed(1, 1)
    make_queries(3, 1)
    swap_queries = start_copy(
        made_queries.at[pl.ds(2 * other, 2)], queries.at[pl.ds(2 * section, 2)],
        swap_s.at[0], swap_r.at[0], section=other,
    )
    own_queries = pltpu.make_async_copy(
        made_queries.at[pl.ds(2 * section, 2)], queries.at[pl.ds(2 * section, 2)], own_s.at[0]
    )
    swap_queries.start()
    own_queries.start()
    climbed(3, 0)
    own_queries.wait()
    swap_queries.wait_recv()

    def token_of(index):
        slot = index // rows
        base = jnp.zeros_like(index)
        for number in range(4):
            base = jnp.where(slot == number, ((place + steps[number]) % 4) * rows, base)
        return base + index % rows

    key_token = token_of(lax.broadcasted_iota(jnp.int32, (1, tokens), 1))
    query_token = shard * tokens + token_of(lax.broadcasted_iota(jnp.int32, (tokens, 1), 0))

    def turn(step):
        if step == 1:
            climbed(0, 2)
            climbed(2, 1)
        elif step == 2:
            spread(2, 0)
            climbed(1, 2)
            for part in range(3):
                pl.when(x > 0)(functools.partial(got_right, part))
                pl.when(x == 3)(functools.partial(got_left, part))
        elif step == 3:
            spread(1, 1)
            spread(0, 2)
        elif step == 5:
            climbed(3, 1)
            climbed(2, 2)
        elif step == 6:
            spread(2, 1)
            climbed(3, 2)
        elif step == 7:
            spread(1, 2)
            late_edge(0)
        elif step == 9:
            for part in range(3):
                passed(0, part)
        elif step == 10:
            spread(2, 2)
            late_edge(1)
            passed(2, 0)
        elif step == 12:
            late_edge(2)
            passed(2, 1)
        elif step == 14:
            for part in range(3):
                passed(1, part)
            passed(2, 2)
        elif step == 16:
            for part in range(3):
                far_up(part).wait_recv()

    def visit(step, carried):
        for number in (1, 2, 3, 5, 6, 7, 9, 10, 12, 14, 16):
            pl.when(step == number)(functools.partial(turn, number))
        keys = meta[0, step] + key_token
        listed = meta[1, step] == 1
        start = jnp.where(listed, starts[:, :1], shard * tokens + tokens)
        seen = (keys >= start) & (keys <= query_token)
        wide[:, :HEAD_WIDTH] = blocks[step, :, HEAD_WIDTH:]
        for head in range(4):
            scores = lax.dot_general(
                queries[head],
                blocks[step, :, :HEAD_WIDTH],
                (((1,), (1,)), ((), ())),
                preferred_element_type=jnp.float32,
            )
            raised = jnp.where(seen, jnp.exp2(jnp.tanh(scores) * RAISE), 0.0)
            total[head] += jnp.dot(
                raised.astype(jnp.bfloat16), wide[...], preferred_element_type=jnp.float32
            )
        return carried

    lax.fori_loop(0, len(SLOTS), visit, 0)

    def swap_back(part):
        span = pl.ds(*BACK[part])
        return start_copy(
            ready.at[span], heads.at[section, span], swap_s.at[1 + part], swap_r.at[1 + part], section=other
        )

    def share_of(owner, low, count, mine):
        value = total[2 * owner + mine, low : low + count, :]
        return (value[:, :HEAD_WIDTH] / value[:, HEAD_WIDTH:]).astype(jnp.bfloat16)

    for part in range(2):
        low, count = BACK[part]
        for mine in range(2):
            lanes = slice(mine * HEAD_WIDTH, (mine + 1) * HEAD_WIDTH)
            ready[low : low + count, lanes] = share_of(other, low, count, mine)
        swap_back(part).start()
    for part in range(2):
        low, count = BACK[part]
        for mine in range(2):
            lanes = slice(mine * HEAD_WIDTH, (mine + 1) * HEAD_WIDTH)
            heads[section, low : low + count, lanes] = share_of(section, low, count, mine)
    fetch_out.wait()
    swap_back(0).wait_recv()

    near_slot = (2, 1)
    inner = 2 * HEAD_WIDTH

    def partial(slot, low):
        span = slice(slot * rows, (slot + 1) * rows)
        return jnp.dot(
            heads[0, span, :], out_weight[:inner, low : low + piece], preferred_element_type=jnp.float32
        ) + jnp.dot(
            heads[1, span, :], out_weight[inner:, low : low + piece], preferred_element_type=jnp.float32
        )

    def send(source, target, sent, landed, side, part):
        return start_copy(
            source.at[side, part], target.at[side, part], sent.at[side, part], landed.at[side, part],
            head=sides[side],
        )

    def far_copy(side, part):
        return send(far_out, far_in, far_s, far_r, side, part)

    def near_copy(side, part):
        return send(near_out, near_in, near_s, near_r, side, part)

    def sum_copy(side, part):
        return send(sum_out, sum_in, sum_s, sum_r, side, part)

    for part in range(PIECES):
        for side in range(2):
            far_out[side, part] = partial(3, side * half + part * piece).astype(jnp.bfloat16)
            far_copy(side, part).start()
    swap_back(1).wait_recv()
    for part in range(PIECES):
        for side in range(2):
            low = (1 - side) * half + part * piece
            near_out[side, part] = partial(near_slot[side], low).astype(jnp.bfloat16)
            near_copy(side, part).start()
    for part in range(PIECES):
        for side in range(2):
            low = side * half + part * piece
            own = partial(near_slot[side], low).astype(jnp.bfloat16).astype(jnp.float32)
            far_copy(side, part).wait_recv()
            sum_out[side, part] = (own + far_in[side, part].astype(jnp.float32)).astype(jnp.bfloat16)
            sum_copy(side, part).start()
    for part in range(2 * PIECES):
        low = part * piece
        mixed[:, low : low + piece] = partial(0, low).astype(jnp.bfloat16).astype(jnp.float32)
    for part in range(PIECES):
        for side in range(2):
            low = (1 - side) * half + part * piece
            near_copy(side, part).wait_recv()
            mixed[:, low : low + piece] += near_in[side, part].astype(jnp.float32)
    squares = jnp.zeros((rows, 128), jnp.float32)
    for part in range(PIECES):
        for side in range(2):
            low = side * half + part * piece
            sum_copy(side, part).wait_recv()
            value = mixed[:, low : low + piece] + sum_in[side, part].astype(jnp.float32)
            mixed[:, low : low + piece] = value
            square = value * value
            for column in range(0, piece, 128):
                squares = squares + square[:, column : column + 128]
    scale = lax.rsqrt(jnp.sum(squares, axis=-1, keepdims=True) / width + epsilon)
    for part in range(2 * PIECES):
        span = slice(part * piece, (part + 1) * piece)
        out_ref[:, span] = (
            hidden_ref[:, span].astype(jnp.float32) + mixed[:, span] * scale * post_ref[:, span]
        ).astype(jnp.bfloat16)

    for side in range(2):
        for part in range(PIECES):
            for kind in range(3):
                row_copy(side, kind, part).wait_send()
            far_copy(side, part).wait_send()
            near_copy(side, part).wait_send()
            sum_copy(side, part).wait_send()
    for part in range(2):
        swap_back(part).wait_send()
    swap_queries.wait_send()
    for part in range(3):
        for step in range(4):
            climb(step, part).wait_send()
        for row in range(3):
            to_right(row, part).wait_send()
            to_left(row, part).wait_send()
            pass_keys(row, part).wait_send()
            pass_values(row, part).wait_send()
        edge_right(0, part).wait_send()
        edge_left(0, part).wait_send()
        far_up(part).wait_send()

    @pl.when(section == 0)
    def _():
        for part in range(3):
            hand_keys(part).wait_send()
        for number in range(3):
            share_across(number).wait_send()
        for at in climbs:
            climb_weights(*at).wait_send()
        for at in second_climbs:
            climb_second(*at).wait_send()
        for back in range(ZS):
            for side in range(2):
                cross_second(side, back).wait_send()
            relay_second(back).wait_send()


def layer(table, hidden, gain, positions, frequency, query_weight, share, out_weight, post_gain):
    rows, width = hidden.shape
    tokens = 4 * rows
    dma = pltpu.SemaphoreType.DMA
    whole = pl.BlockSpec(memory_space=pltpu.VMEM)
    apart = pl.BlockSpec(memory_space=pl.ANY)
    small = pl.BlockSpec(memory_space=pltpu.SMEM)
    pieces = pltpu.VMEM((2, PIECES, rows, width // (2 * PIECES)), jnp.bfloat16)

    def half_type(*shape):
        return pltpu.VMEM(shape, jnp.bfloat16)

    pair = 2 * HEAD_WIDTH
    return pl.pallas_call(
        layer_kernel,
        out_shape=jax.ShapeDtypeStruct((rows, width), jnp.bfloat16),
        in_specs=[small, whole, whole, whole, whole, apart, whole, apart, whole],
        out_specs=whole,
        scratch_shapes=[
            pltpu.SMEM((2, len(SLOTS)), jnp.int32),
            half_type(4, rows, width),
            half_type(*query_weight.shape),
            half_type(width, share.shape[1] * share.shape[2]),
            half_type(*out_weight.shape),
            half_type(4, tokens, HEAD_WIDTH),
            half_type(2, tokens, pair),
            half_type(4, tokens, HEAD_WIDTH),
            half_type(len(SLOTS), tokens, pair),
            pltpu.VMEM((tokens, HEAD_WIDTH), jnp.int32),
            pltpu.VMEM((tokens, HEAD_WIDTH), jnp.float32),
            pltpu.VMEM((tokens, HEAD_WIDTH), jnp.float32),
            pltpu.VMEM((4, tokens, pair), jnp.float32),
            half_type(tokens, pair),
            half_type(tokens, pair),
            half_type(2, tokens, pair),
            pieces, pieces, pieces, pieces, pieces, pieces,
            pltpu.VMEM((rows, width), jnp.float32),
            dma((2,)), dma((2, 3, PIECES)), dma((2, 3, PIECES)), dma((3,)), dma((3,)),
            dma((2, 4, 4)), dma((2, 4, 4)), dma((2, 4)), dma((2, 4)), dma((2, ZS)), dma((2, ZS)), dma((ZS,)), dma((ZS,)),
            dma((3,)), dma((3,)), dma((4,)), dma((3,)), dma((3,)),
            dma((4, 3)), dma((4, 3)), dma((4, 3)), dma((4, 3)), dma((4, 3)), dma((4, 3)),
            dma((3, 3)), dma((3, 3)), dma((3, 3)), dma((3, 3)), dma((3,)), dma((3,)),
        ]
        + [dma((2, PIECES))] * 6,
        compiler_params=pltpu.CompilerParams(
            collective_id=1, has_side_effects=True, vmem_limit_bytes=62 * 2**20
        ),
        name="layer",
    )(table, hidden, gain, positions, frequency, query_weight, share, out_weight, post_gain)


def local(hidden, q_weight, key_value_weight, o_weight, in_gain, post_gain, positions, block_table):
    lane = np.arange(HEAD_WIDTH) % (HEAD_WIDTH // 2)
    frequency = jnp.asarray((10000.0 ** (-lane * 2.0 / HEAD_WIDTH)).astype(np.float32))
    return layer(
        block_table, hidden[0], in_gain, positions.reshape(-1, hidden.shape[1]), frequency[None],
        q_weight[0], key_value_weight, o_weight[0], post_gain,
    )[None]


def solution(mesh):
    placed = (
        P("section", ("seq", "head"), None),
        P("section", None, "head"),
        P("seq", None, "head"),
        P("section", "head", None),
        P("section", None),
        P("section", None),
        P(),
        P(),
    )
    return jax.shard_map(
        local,
        mesh=mesh,
        in_specs=placed,
        out_specs=P("section", ("seq", "head"), None),
        check_vma=False,
    )
```

```python
import math

import functools

import jax
import jax.numpy as jnp
import numpy as np
from jax import lax
from jax.experimental import pallas as pl
from jax.experimental.pallas import tpu as pltpu
from jax.sharding import PartitionSpec as P

HEAD_WIDTH = 128


epsilon = 1e-06
softcap_limit = 50.0
query_scale = 144.0 ** (-0.5)
RAISE = softcap_limit * math.log2(math.e)
XS, ZS = 4, 8


SLOTS = (
    (0, 0), (1, 0), (2, 0), (1, 1), (1, 3), (3, 0), (4, 0), (2, 1), (2, 3),
    (1, 2), (3, 1), (3, 3), (-1, 1), (-1, 3), (2, 2), (3, 2), (-1, 2),
)
PARTS = ((0, 128), (128, 256), (384, 128))
BACK = ((384, 128), (0, 384))
FIRST = 64
PIECES = 3


def start_copy(source, target, sent, landed, **place):
    copy = pltpu.make_async_remote_copy(
        src_ref=source,
        dst_ref=target,
        send_sem=sent,
        recv_sem=landed,
        device_id=place,
        device_id_type=pl.DeviceIdType.MESH,
    )
    return copy


def greet(places):
    barrier = pltpu.get_barrier_semaphore()
    for place in places:
        pl.semaphore_signal(
            barrier, inc=1, device_id=place, device_id_type=pl.DeviceIdType.MESH
        )
    pl.semaphore_wait(barrier, len(places))


def layer_kernel(
    table, hidden_ref, gain_ref, position_ref, frequency_ref, query_hbm, share_ref, out_hbm, post_ref, out_ref,
    meta, normed, query_weight, kv_weight, out_weight, made_queries, made_kv, queries, blocks, starts, cosine, sine,
    total, wide, ready, heads, far_out, near_out, sum_out, far_in, near_in, sum_in, mixed,
    load, side_s, side_r, x_s, x_r, w_s, w_r, b_s, b_r, c_s, c_r, d_s, d_r, swap_s, swap_r, own_s, hand_s, hand_r,
    z_s, z_r, right_s, right_r, left_s, left_r, key_s, key_r, value_s, value_r, edge_s, edge_r,
    far_s, far_r, near_s, near_r, sum_s, sum_r,
):
    section = lax.axis_index("section")
    shard = lax.axis_index("seq")
    place = lax.axis_index("head")
    other = 1 - section
    z, x = shard // XS, shard % XS
    up = ((z + 1) % ZS) * XS + x
    down = ((z + ZS - 1) % ZS) * XS + x
    across = [z * XS + (x + step) % XS for step in (1, 3, 2)]
    right, left = across[0], across[1]
    rows, width = hidden_ref.shape
    tokens = 4 * rows
    half = width // 2
    piece = half // PIECES
    depth = share_ref.shape[0]
    sides = ((place + 1) % 4, (place + 3) % 4)
    steps = (0, 3, 1, 2)
    fetch = pltpu.make_async_copy(query_hbm, query_weight, load.at[0])
    fetch.start()
    fetch_out = pltpu.make_async_copy(out_hbm, out_weight, load.at[1])
    own_share = pl.ds(pl.multiple_of(shard * depth, 16), depth)
    columns = share_ref.shape[2]
    for number in range(2):
        kv_weight[own_share, number * columns : (number + 1) * columns] = share_ref[:, number, :]
    greet(
        [{"head": sides[0]}, {"head": sides[1]}, {"section": other}]
        + [{"seq": seq} for seq in across + [up, down]]
    )

    def weight_rows(zz, xx, second):
        low = (zz * XS + xx) * depth + (FIRST if second else 0)
        return pl.ds(pl.multiple_of(low, 16), depth - FIRST if second else FIRST)

    def weight_copy(zz, xx, second, sent, landed, seq):
        span = weight_rows(zz % ZS, xx % XS, second)
        return start_copy(kv_weight.at[span], kv_weight.at[span], sent, landed, seq=seq)

    def share_across(number):
        return weight_copy(z, x, False, x_s.at[number], x_r.at[number], across[number])

    def climb_weights(side, hop, aside):
        origin = z + ZS - (hop - 1) if side == 0 else z + (hop - 1)
        return weight_copy(
            origin, x + aside, False, w_s.at[side, hop - 1, aside], w_r.at[side, hop - 1, aside], (up, down)[side]
        )

    climbs = [
        (side, hop, aside)
        for hop in range(1, 5)
        for aside in range(4)
        for side in range(2)
        if hop < 4 or (aside < 2) == (side == 0)
    ]

    def climb_second(side, hop):
        origin = z + ZS - (hop - 1) if side == 0 else z + (hop - 1)
        return weight_copy(origin, x, True, b_s.at[side, hop - 1], b_r.at[side, hop - 1], (up, down)[side])

    second_climbs = [(side, hop) for hop in range(1, 5) for side in range(2) if hop < 4 or side == 0]

    def cross_second(side, back):
        return weight_copy(
            z + ZS - back, x, True, c_s.at[side, back], c_r.at[side, back], (right, left)[side]
        )

    def relay_second(back):
        side = back % 2
        return weight_copy(
            z + ZS - back, x + (3, 1)[side], True, d_s.at[back], d_r.at[back], (right, left)[side]
        )

    def row_copy(side, kind, part):
        which = side if kind == 0 else 1 - side
        span = pl.ds((side if kind == 2 else which) * half + part * piece, piece)
        source = (0, 0, 1 + side)[kind]
        target = (1 + side, 1 + side, 3)[kind]
        return start_copy(
            normed.at[source, :, span], normed.at[target, :, span],
            side_s.at[side, kind, part], side_r.at[side, kind, part], head=sides[side],
        )

    @pl.when(section == 0)
    def _():
        for number in range(3):
            share_across(number).start()
        for side in range(2):
            climb_second(side, 1).start()
            climb_weights(side, 1, 0).start()
            cross_second(side, 0).start()

    squares = jnp.zeros((rows, 128), jnp.float32)
    for column in range(0, width, 128):
        value = hidden_ref[:, column : column + 128].astype(jnp.float32)
        squares = squares + value * value
    scale = lax.rsqrt(jnp.sum(squares, axis=-1, keepdims=True) / width + epsilon)
    for part in range(2 * PIECES):
        span = slice(part * piece, (part + 1) * piece)
        normed[0, :, span] = (
            hidden_ref[:, span].astype(jnp.float32) * scale * gain_ref[:, span]
        ).astype(jnp.bfloat16)
    for kind in range(2):
        for part in range(PIECES):
            for side in range(2):
                row_copy(side, kind, part).start()

    @pl.when(section == 0)
    def _():
        for number, aside in ((0, 3), (1, 1), (2, 2)):
            share_across(number).wait_recv()
            for side in range(2):
                climb_weights(side, 1, aside).start()

    for number, (back, aside) in enumerate(SLOTS):
        source = (x + XS - aside) % XS
        row = jnp.where(source < x, 0, 4) if back < 0 else back
        block = (z - row) * XS + source
        meta[0, number] = block * tokens
        meta[1, number] = table[shard, jnp.maximum(block, 0)]
    def product(first, count, weight, low):
        return jnp.dot(
            normed[first : first + count].reshape(count * rows, width),
            weight[:, low : low + 2 * HEAD_WIDTH],
            preferred_element_type=jnp.float32,
        )

    def turned(value, span):
        return value * cosine[span, :] + pltpu.roll(value, HEAD_WIDTH // 2, 1) * sine[span, :]

    def make_queries(first, count):
        for pair in range(2):
            result = product(first, count, query_weight, pair * 2 * HEAD_WIDTH)
            for slot in range(count):
                low = (first + slot) * rows
                for mine in range(2):
                    value = result[slot * rows : (slot + 1) * rows, mine * HEAD_WIDTH : (mine + 1) * HEAD_WIDTH]
                    made_queries[2 * pair + mine, low : low + rows, :] = (
                        turned(value, slice(low, low + rows)) * (query_scale / softcap_limit)
                    ).astype(jnp.bfloat16)

    def make_keys(first, count):
        for pair in range(2):
            result = product(first, count, kv_weight, pair * 2 * HEAD_WIDTH)
            for slot in range(count):
                low = (first + slot) * rows
                for mine in range(2):
                    value = result[slot * rows : (slot + 1) * rows, mine * HEAD_WIDTH : (mine + 1) * HEAD_WIDTH]
                    if pair == 0:
                        value = turned(value, slice(low, low + rows))
                    made_kv[mine, low : low + rows, pair * HEAD_WIDTH : (pair + 1) * HEAD_WIDTH] = value.astype(
                        jnp.bfloat16
                    )

    def pass_weights(hop):
        @pl.when(section == 0)
        def _():
            for side, at in second_climbs:
                if at == hop:
                    climb_second(side, hop).wait_recv()
                    if (side, hop + 1) in second_climbs:
                        climb_second(side, hop + 1).start()
                    for across_side in range(2):
                        cross_second(across_side, hop if side == 0 else ZS - hop).start()
            for side, at, aside in climbs:
                if at == hop:
                    climb_weights(side, hop, aside).wait_recv()
                    if (side, hop + 1, aside) in climbs:
                        climb_weights(side, hop + 1, aside).start()
            for back in ((0,), (1, 7), (2, 6), (3, 5), (4,))[hop - 1]:
                for side in range(2):
                    cross_second(side, back).wait_recv()
                relay_second(back).start()

    def finish_weights():
        for side in range(2):
            cross_second(side, 4).wait_recv()
        relay_second(4).start()
        for back in range(ZS):
            relay_second(back).wait_recv()

    def span_of(part):
        return pl.ds(*PARTS[part])

    def hand_keys(part):
        span = span_of(part)
        return start_copy(
            made_kv.at[1, span], blocks.at[0, span], hand_s.at[part], hand_r.at[part], section=other
        )

    def own_keys(part):
        span = span_of(part)
        return pltpu.make_async_copy(made_kv.at[0, span], blocks.at[0, span], own_s.at[1 + part])

    def block_copy(source, target, part, sent, landed, seq, columns=(0, 2 * HEAD_WIDTH)):
        span, width_of = span_of(part), pl.ds(*columns)
        return start_copy(
            blocks.at[source, span, width_of], blocks.at[target, span, width_of], sent, landed, seq=seq
        )

    def climb(step, part):
        slots = (0, 1, 2, 5, 6)
        return block_copy(slots[step], slots[step + 1], part, z_s.at[step, part], z_r.at[step, part], up)

    def to_right(row, part):
        source, target = ((1, 3), (2, 7), (5, 10))[row]
        return block_copy(source, target, part, right_s.at[row, part], right_r.at[row, part], right)

    def to_left(row, part):
        source, target = ((1, 4), (2, 8), (5, 11))[row]
        return block_copy(source, target, part, left_s.at[row, part], left_r.at[row, part], left)

    keys_of, values_of = (0, HEAD_WIDTH), (HEAD_WIDTH, HEAD_WIDTH)

    def pass_keys(row, part):
        source, target = ((3, 9), (7, 14), (10, 15))[row]
        return block_copy(source, target, part, key_s.at[row, part], key_r.at[row, part], right, keys_of)

    def pass_values(row, part):
        source, target = ((4, 9), (8, 14), (11, 15))[row]
        return block_copy(source, target, part, value_s.at[row, part], value_r.at[row, part], left, values_of)

    def edge_right(source, part):
        return block_copy(source, 12, part, right_s.at[3, part], right_r.at[3, part], right)

    def edge_left(source, part):
        return block_copy(source, 13, part, left_s.at[3, part], left_r.at[3, part], left)

    def edge_far(kind, part):
        return block_copy(
            (12, 12, 13, 13)[kind], 16, part, edge_s.at[kind, part], edge_r.at[kind % 2, part],
            (right, right, left, left)[kind], (keys_of, values_of)[kind % 2],
        )

    far_when = (x < 3, x == 2, x == 1, x > 0)

    def begin(part):
        climb(0, part).start()
        pl.when(x < 3)(lambda: edge_right(0, part).start())
        pl.when(x == 0)(lambda: edge_left(0, part).start())

    def climbed(step, part):
        climb(step, part).wait_recv()
        if step < 3:
            climb(step + 1, part).start()
            to_right(step, part).start()
            to_left(step, part).start()
        else:
            pl.when(x == 3)(lambda: edge_right(6, part).start())
            pl.when(x > 0)(lambda: edge_left(6, part).start())

    def spread(row, part):
        to_right(row, part).wait_recv()
        pass_keys(row, part).start()
        to_left(row, part).wait_recv()
        pass_values(row, part).start()

    def passed(row):
        for part in range(3):
            pass_keys(row, part).wait_recv()
            pass_values(row, part).wait_recv()

    def got_right(part):
        edge_right(0, part).wait_recv()
        for kind in (0, 1):
            pl.when(far_when[kind])(edge_far(kind, part).start)

    def got_left(part):
        edge_left(0, part).wait_recv()
        for kind in (2, 3):
            pl.when(far_when[kind])(edge_far(kind, part).start)

    def late_edge(part):
        pl.when(x == 0)(lambda: got_right(part))
        pl.when(x < 3)(lambda: got_left(part))

    def give_keys(part, first, count):
        @pl.when(section == 0)
        def _():
            make_keys(first, count)
            hand_keys(part).start()
            own_keys(part).start()
            own_keys(part).wait()

        pl.when(section == 1)(lambda: hand_keys(part).wait_recv())
        begin(part)

    pass_weights(1)
    pass_weights(2)
    lane = lax.broadcasted_iota(jnp.int32, (rows, HEAD_WIDTH), 1)
    line = lax.broadcasted_iota(jnp.int32, (rows, HEAD_WIDTH), 0)
    for slot in range(4):
        origin = (place + steps[slot]) % 4
        span = slice(slot * rows, (slot + 1) * rows)
        at = jnp.transpose(jnp.broadcast_to(position_ref[pl.ds(4 * shard + origin, 1), :], (rows, rows)))
        starts[span, :] = shard * tokens + origin * rows + line - at
        angle = at.astype(jnp.float32) * frequency_ref[...]
        cosine[span, :] = jnp.cos(angle)
        sine[span, :] = jnp.sin(angle) * jnp.where(lane < HEAD_WIDTH // 2, -1.0, 1.0)
    pass_weights(3)
    for part in range(PIECES):
        for side in range(2):
            row_copy(side, 0, part).wait_recv()
            row_copy(side, 2, part).start()
    pass_weights(4)
    pl.when(section == 0)(finish_weights)
    give_keys(0, 0, 1)
    fetch.wait()
    make_queries(0, 1)
    total[...] = jnp.zeros_like(total)
    wide[...] = jnp.ones_like(wide)

    for part in range(PIECES):
        for side in range(2):
            row_copy(side, 1, part).wait_recv()
    climbed(0, 0)
    pl.when(section == 1)(lambda: make_queries(1, 2))
    give_keys(1, 1, 2)
    spread(0, 0)
    climbed(1, 0)
    fetch_out.start()
    for part in range(PIECES):
        for side in range(2):
            row_copy(side, 2, part).wait_recv()
    give_keys(2, 3, 1)
    climbed(2, 0)
    climbed(0, 1)
    spread(1, 0)
    pl.when(section == 0)(lambda: make_queries(1, 2))
    spread(0, 1)
    climbed(1, 1)
    make_queries(3, 1)
    swap_queries = start_copy(
        made_queries.at[pl.ds(2 * other, 2)], queries.at[pl.ds(2 * section, 2)],
        swap_s.at[0], swap_r.at[0], section=other,
    )
    own_queries = pltpu.make_async_copy(
        made_queries.at[pl.ds(2 * section, 2)], queries.at[pl.ds(2 * section, 2)], own_s.at[0]
    )
    swap_queries.start()
    own_queries.start()
    climbed(3, 0)
    own_queries.wait()
    swap_queries.wait_recv()

    def token_of(index):
        slot = index // rows
        base = jnp.zeros_like(index)
        for number in range(4):
            base = jnp.where(slot == number, ((place + steps[number]) % 4) * rows, base)
        return base + index % rows

    key_token = token_of(lax.broadcasted_iota(jnp.int32, (1, tokens), 1))
    query_token = shard * tokens + token_of(lax.broadcasted_iota(jnp.int32, (tokens, 1), 0))

    def turn(step):
        if step == 1:
            climbed(0, 2)
            climbed(2, 1)
        elif step == 2:
            spread(2, 0)
            climbed(1, 2)
            for part in range(3):
                pl.when(x > 0)(functools.partial(got_right, part))
                pl.when(x == 3)(functools.partial(got_left, part))
        elif step == 3:
            spread(1, 1)
            spread(0, 2)
        elif step == 5:
            climbed(3, 1)
            climbed(2, 2)
        elif step == 6:
            spread(2, 1)
            climbed(3, 2)
        elif step == 7:
            spread(1, 2)
            late_edge(0)
        elif step == 9:
            passed(0)
        elif step == 10:
            spread(2, 2)
            late_edge(1)
        elif step == 12:
            late_edge(2)
        elif step == 14:
            passed(1)
        elif step == 15:
            passed(2)
        elif step == 16:
            for part in range(3):
                for kind in range(2):
                    edge_far(kind, part).wait_recv()

    def visit(step, carried):
        for number in (1, 2, 3, 5, 6, 7, 9, 10, 12, 14, 15, 16):
            pl.when(step == number)(functools.partial(turn, number))
        keys = meta[0, step] + key_token
        listed = meta[1, step] == 1
        start = jnp.where(listed, starts[:, :1], shard * tokens + tokens)
        seen = (keys >= start) & (keys <= query_token)
        wide[:, :HEAD_WIDTH] = blocks[step, :, HEAD_WIDTH:]
        for head in range(4):
            scores = lax.dot_general(
                queries[head],
                blocks[step, :, :HEAD_WIDTH],
                (((1,), (1,)), ((), ())),
                preferred_element_type=jnp.float32,
            )
            raised = jnp.where(seen, jnp.exp2(jnp.tanh(scores) * RAISE), 0.0)
            total[head] += jnp.dot(
                raised.astype(jnp.bfloat16), wide[...], preferred_element_type=jnp.float32
            )
        return carried

    lax.fori_loop(0, len(SLOTS), visit, 0)

    def swap_back(part):
        span = pl.ds(*BACK[part])
        return start_copy(
            ready.at[span], heads.at[section, span], swap_s.at[1 + part], swap_r.at[1 + part], section=other
        )

    def share_of(owner, low, count, mine):
        value = total[2 * owner + mine, low : low + count, :]
        return (value[:, :HEAD_WIDTH] / value[:, HEAD_WIDTH:]).astype(jnp.bfloat16)

    for part in range(2):
        low, count = BACK[part]
        for mine in range(2):
            lanes = slice(mine * HEAD_WIDTH, (mine + 1) * HEAD_WIDTH)
            ready[low : low + count, lanes] = share_of(other, low, count, mine)
        swap_back(part).start()
    for part in range(2):
        low, count = BACK[part]
        for mine in range(2):
            lanes = slice(mine * HEAD_WIDTH, (mine + 1) * HEAD_WIDTH)
            heads[section, low : low + count, lanes] = share_of(section, low, count, mine)
    fetch_out.wait()
    swap_back(0).wait_recv()

    near_slot = (2, 1)
    inner = 2 * HEAD_WIDTH

    def partial(slot, low):
        span = slice(slot * rows, (slot + 1) * rows)
        return jnp.dot(
            heads[0, span, :], out_weight[:inner, low : low + piece], preferred_element_type=jnp.float32
        ) + jnp.dot(
            heads[1, span, :], out_weight[inner:, low : low + piece], preferred_element_type=jnp.float32
        )

    def send(source, target, sent, landed, side, part):
        return start_copy(
            source.at[side, part], target.at[side, part], sent.at[side, part], landed.at[side, part],
            head=sides[side],
        )

    def far_copy(side, part):
        return send(far_out, far_in, far_s, far_r, side, part)

    def near_copy(side, part):
        return send(near_out, near_in, near_s, near_r, side, part)

    def sum_copy(side, part):
        return send(sum_out, sum_in, sum_s, sum_r, side, part)

    for part in range(PIECES):
        for side in range(2):
            far_out[side, part] = partial(3, side * half + part * piece).astype(jnp.bfloat16)
            far_copy(side, part).start()
    swap_back(1).wait_recv()
    for part in range(PIECES):
        for side in range(2):
            low = (1 - side) * half + part * piece
            near_out[side, part] = partial(near_slot[side], low).astype(jnp.bfloat16)
            near_copy(side, part).start()
    for part in range(PIECES):
        for side in range(2):
            low = side * half + part * piece
            own = partial(near_slot[side], low).astype(jnp.bfloat16).astype(jnp.float32)
            far_copy(side, part).wait_recv()
            sum_out[side, part] = (own + far_in[side, part].astype(jnp.float32)).astype(jnp.bfloat16)
            sum_copy(side, part).start()
    for part in range(2 * PIECES):
        low = part * piece
        mixed[:, low : low + piece] = partial(0, low).astype(jnp.bfloat16).astype(jnp.float32)
    for part in range(PIECES):
        for side in range(2):
            low = (1 - side) * half + part * piece
            near_copy(side, part).wait_recv()
            mixed[:, low : low + piece] += near_in[side, part].astype(jnp.float32)
    squares = jnp.zeros((rows, 128), jnp.float32)
    for part in range(PIECES):
        for side in range(2):
            low = side * half + part * piece
            sum_copy(side, part).wait_recv()
            value = mixed[:, low : low + piece] + sum_in[side, part].astype(jnp.float32)
            mixed[:, low : low + piece] = value
            square = value * value
            for column in range(0, piece, 128):
                squares = squares + square[:, column : column + 128]
    scale = lax.rsqrt(jnp.sum(squares, axis=-1, keepdims=True) / width + epsilon)
    for part in range(2 * PIECES):
        span = slice(part * piece, (part + 1) * piece)
        out_ref[:, span] = (
            hidden_ref[:, span].astype(jnp.float32) + mixed[:, span] * scale * post_ref[:, span]
        ).astype(jnp.bfloat16)

    for side in range(2):
        for part in range(PIECES):
            for kind in range(3):
                row_copy(side, kind, part).wait_send()
            far_copy(side, part).wait_send()
            near_copy(side, part).wait_send()
            sum_copy(side, part).wait_send()
    for part in range(2):
        swap_back(part).wait_send()
    swap_queries.wait_send()
    for part in range(3):
        for step in range(4):
            climb(step, part).wait_send()
        for row in range(3):
            to_right(row, part).wait_send()
            to_left(row, part).wait_send()
            pass_keys(row, part).wait_send()
            pass_values(row, part).wait_send()
        edge_right(0, part).wait_send()
        edge_left(0, part).wait_send()
        for kind in range(4):
            pl.when(far_when[kind])(edge_far(kind, part).wait_send)

    @pl.when(section == 0)
    def _():
        for part in range(3):
            hand_keys(part).wait_send()
        for number in range(3):
            share_across(number).wait_send()
        for at in climbs:
            climb_weights(*at).wait_send()
        for at in second_climbs:
            climb_second(*at).wait_send()
        for back in range(ZS):
            for side in range(2):
                cross_second(side, back).wait_send()
            relay_second(back).wait_send()


def layer(table, hidden, gain, positions, frequency, query_weight, share, out_weight, post_gain):
    rows, width = hidden.shape
    tokens = 4 * rows
    dma = pltpu.SemaphoreType.DMA
    whole = pl.BlockSpec(memory_space=pltpu.VMEM)
    apart = pl.BlockSpec(memory_space=pl.ANY)
    small = pl.BlockSpec(memory_space=pltpu.SMEM)
    pieces = pltpu.VMEM((2, PIECES, rows, width // (2 * PIECES)), jnp.bfloat16)

    def half_type(*shape):
        return pltpu.VMEM(shape, jnp.bfloat16)

    pair = 2 * HEAD_WIDTH
    return pl.pallas_call(
        layer_kernel,
        out_shape=jax.ShapeDtypeStruct((rows, width), jnp.bfloat16),
        in_specs=[small, whole, whole, whole, whole, apart, whole, apart, whole],
        out_specs=whole,
        scratch_shapes=[
            pltpu.SMEM((2, len(SLOTS)), jnp.int32),
            half_type(4, rows, width),
            half_type(*query_weight.shape),
            half_type(width, share.shape[1] * share.shape[2]),
            half_type(*out_weight.shape),
            half_type(4, tokens, HEAD_WIDTH),
            half_type(2, tokens, pair),
            half_type(4, tokens, HEAD_WIDTH),
            half_type(len(SLOTS), tokens, pair),
            pltpu.VMEM((tokens, HEAD_WIDTH), jnp.int32),
            pltpu.VMEM((tokens, HEAD_WIDTH), jnp.float32),
            pltpu.VMEM((tokens, HEAD_WIDTH), jnp.float32),
            pltpu.VMEM((4, tokens, pair), jnp.float32),
            half_type(tokens, pair),
            half_type(tokens, pair),
            half_type(2, tokens, pair),
            pieces, pieces, pieces, pieces, pieces, pieces,
            pltpu.VMEM((rows, width), jnp.float32),
            dma((2,)), dma((2, 3, PIECES)), dma((2, 3, PIECES)), dma((3,)), dma((3,)),
            dma((2, 4, 4)), dma((2, 4, 4)), dma((2, 4)), dma((2, 4)), dma((2, ZS)), dma((2, ZS)), dma((ZS,)), dma((ZS,)),
            dma((3,)), dma((3,)), dma((4,)), dma((3,)), dma((3,)),
            dma((4, 3)), dma((4, 3)), dma((4, 3)), dma((4, 3)), dma((4, 3)), dma((4, 3)),
            dma((3, 3)), dma((3, 3)), dma((3, 3)), dma((3, 3)), dma((4, 3)), dma((2, 3)),
        ]
        + [dma((2, PIECES))] * 6,
        compiler_params=pltpu.CompilerParams(
            collective_id=1, has_side_effects=True, vmem_limit_bytes=62 * 2**20
        ),
        name="layer",
    )(table, hidden, gain, positions, frequency, query_weight, share, out_weight, post_gain)


def local(hidden, q_weight, key_value_weight, o_weight, in_gain, post_gain, positions, block_table):
    lane = np.arange(HEAD_WIDTH) % (HEAD_WIDTH // 2)
    frequency = jnp.asarray((10000.0 ** (-lane * 2.0 / HEAD_WIDTH)).astype(np.float32))
    return layer(
        block_table, hidden[0], in_gain, positions.reshape(-1, hidden.shape[1]), frequency[None],
        q_weight[0], key_value_weight, o_weight[0], post_gain,
    )[None]


def solution(mesh):
    placed = (
        P("section", ("seq", "head"), None),
        P("section", None, "head"),
        P("seq", None, "head"),
        P("section", "head", None),
        P("section", None),
        P("section", None),
        P(),
        P(),
    )
    return jax.shard_map(
        local,
        mesh=mesh,
        in_specs=placed,
        out_specs=P("section", ("seq", "head"), None),
        check_vma=False,
    )
```
